512 devices in a mesh: aa: 16 (over z_hi, x), ba: 32 (over z_lo, y, core).
Axes of the slice: x: 4, y: 4, z: 16 (z_hi: 4, z_lo: 4; z = z_hi * 4 + z_lo), core: 2. Of those that a mesh axis runs over, the one named last changes fastest.
Arguments:
- amplitudes: float32 [256, 256, 1024], P('aa', 'ba'), may hold values from -4 to 4
- driving: bfloat16 [256, 256, 1024], P('aa', 'ba'), may hold values from -6 to 6
- ladder: bfloat16 [1024, 1024], P('aa', 'ba'), may hold values from -0.09375 to 0.09375
- block_mask: int32 [16, 16], replicated, may hold values 0 or 1
- virt_energy: float32 [256], replicated, may hold values from 0.5 to 3
- occ_energy: float32 [32], replicated, may hold values from -3 to -0.5
Outputs:
- updated: float32 [256, 256, 1024], P('aa', 'ba')
The draws below stay inside these ranges and needn't reach their ends.
All inputs are finite; a program needn't handle non-finite values.
Results may differ from the reference program's by a relative error of at most 0.0003.
Values may be sent and summed in bfloat16 or wider, within the bound.
A program may use at most 64 MiB of HBM per device.

```python
import jax
import jax.numpy as jnp
from jax import lax

V = 256
O = 32
BLOCK = 64
ITERS = 2
IJ = 1024
NB = 16


def touch_ends(drawn, own_key, smallest, top_value):
    place = [jax.random.randint(jax.random.fold_in(own_key, axis), (), 0, length) for axis, length in enumerate(drawn.shape)]
    widest = drawn.shape.index(max(drawn.shape))
    next_to = place[:widest] + [(place[widest] + 1) % drawn.shape[widest]] + place[widest + 1:]
    return drawn.at[tuple(place)].set(smallest).at[tuple(next_to)].set(top_value)


def levels(own_key, shape, pieces, least, top_value):
    level, own = 1.0, jax.random.fold_in(own_key, 6)
    for axis_at, parts in pieces:
        draws = jnp.exp(jax.random.uniform(jax.random.fold_in(own, axis_at), (parts,), jnp.float32, least / len(pieces), top_value / len(pieces)))
        level = level * jnp.repeat(draws, shape[axis_at] // parts).reshape([-1 if axis == axis_at else 1 for axis in range(len(shape))])
    return level


def normal_values(own_key, extent, spread, most, pieces=(), held_as=jnp.bfloat16):
    entries = spread * jax.random.normal(own_key, extent, jnp.float32)
    if pieces:
        entries = entries * levels(own_key, extent, pieces, -0.22, 0.18)
    return jnp.clip(entries, -most, most).astype(held_as)


def setup_inputs(seed: int = 0) -> dict:
    splits = jax.random.split(jax.random.key(seed), 7)
    return {
        "amplitudes": normal_values(splits[0], (V, V, IJ), 0.3, 4.0, ((0, 16), (1, 32)), jnp.float32),
        "driving": normal_values(splits[1], (V, V, IJ), 1.0, 6.0, ((0, 16), (1, 32))),
        "ladder": normal_values(splits[2], (IJ, IJ), (4 * IJ) ** -0.5, 0.09375, ((0, 16), (1, 32))),
        "block_mask": touch_ends((jax.random.randint(splits[3], (NB, NB), 0, 2) < 1).astype(jnp.int32), jax.random.fold_in(splits[3], 1), 0, 1),
        "virt_energy": jnp.clip(jax.random.uniform(splits[4], (V,), jnp.float32, 0.5, 3.0), 0.5, 3.0),
        "occ_energy": jnp.clip(jax.random.uniform(splits[5], (O,), jnp.float32, -3.0, -0.5), -3.0, -0.5),
    }


def reference(amplitudes, driving, ladder, block_mask, virt_energy, occ_energy):
    blocks = IJ // BLOCK
    kept = block_mask.astype(jnp.float32)[:, None, :, None]
    weights = (ladder.astype(jnp.float32).reshape(blocks, BLOCK, blocks, BLOCK) * kept).reshape(IJ, IJ)
    pair_energy = (occ_energy[:, None] + occ_energy[None, :]).reshape(IJ)
    denominator = virt_energy[:, None, None] + virt_energy[None, :, None] - pair_energy[None, None, :]
    driving_wide = driving.astype(jnp.float32)
    for iteration in range(ITERS):
        ladder_term = jnp.dot(amplitudes.reshape(V * V, IJ), weights, precision=lax.Precision.HIGHEST, preferred_element_type=jnp.float32).reshape(V, V, IJ)
        partner = ladder_term.reshape(V, V, O, O).transpose(1, 0, 3, 2).reshape(V, V, IJ)
        amplitudes = (driving_wide + ladder_term + partner) / denominator
    return amplitudes
```

```python
import functools

import jax
import jax.numpy as jnp
from jax import lax
from jax.experimental import pallas as pl
from jax.experimental.pallas import tpu as pltpu
from jax.sharding import PartitionSpec as P

MESH = pl.DeviceIdType.MESH
F32 = jnp.float32
BF16 = jnp.bfloat16
O = 32
NX = 4
NH = 4
NZ = 16
IJ = 1024
ROWS = 128
COLS = 256
LAG1 = 5
LAG2 = 10


def iota(shape, dim):
    return lax.broadcasted_iota(jnp.int32, shape, dim)


def onehot(cond):
    return jnp.where(cond, 1.0, 0.0).astype(BF16)


def dot(a, b):
    return jnp.dot(a, b, preferred_element_type=F32)


def kernel(
    amp, drv, lad, mask, ve, oe, out,
    G, W, perm, shuf, blk, rden, ab, tb, lhs, x1, x2b, zsend, zrecv, vs,
    z_ss, z_rs, f_ss, f_rs, s_ss, s_rs, c_ss, c_rs, e_ss, e_rs,
):
    p = lax.axis_index("aa")
    q = lax.axis_index("ba")
    zh, x = lax.div(p, NX), lax.rem(p, NX)
    zl = lax.div(q, 2 * NX)
    y = lax.rem(lax.div(q, 2), NX)
    k = lax.rem(q, 2)
    z = zh * NH + zl

    def dev(z_, x_, y_, k_):
        return (lax.div(z_, NH) * NX + x_, lax.rem(z_, NH) * (2 * NX) + y_ * 2 + k_)

    def rot(v, d, n):
        return lax.rem(v + d, n)

    x_peers = [dev(z, rot(x, d, NX), y, k) for d in (1, 3, 2)]
    y_peers = [dev(z, x, rot(y, d, NX), k) for d in (1, 3, 2)]
    sibling = dev(z, x, y, 1 - k)
    z_peer = {d: dev(rot(z, d, NZ), x, y, k) for d in range(1, NZ)}

    barrier = pltpu.get_barrier_semaphore()
    order = [8, 7, 9, 6, 10, 5, 11, 4, 12, 3, 13, 2, 14, 1, 15]
    peers = [z_peer[d] for d in order] + x_peers + y_peers + [sibling]
    for peer in peers:
        pl.semaphore_signal(barrier, inc=1, device_id=peer, device_id_type=MESH)

    keep = mask[p, lax.div(q, 2)].astype(F32)
    packed = jnp.zeros((16, 128), F32)
    for t in range(4):
        place = onehot(iota((32, 128), 1) == iota((32, 128), 0) + 32 * t)
        packed = packed + dot(lad[16 * t : 16 * t + 16, :], place)
    blk[...] = (packed * keep).astype(BF16)
    G[zh, zl, x, y, k] = blk[...]

    def prepare():
        @pl.loop(0, 8)
        def _(i):
            r = iota((128, IJ), 0) + i * 128
            c = iota((128, IJ), 1)
            perm[pl.ds(pl.multiple_of(i * 128, 128), 128), :] = onehot(
                r == (c & (O - 1)) * O + (c >> 5)
            )

        r = iota((512, 512), 0)
        c = iota((512, 512), 1)
        shuf[...] = onehot(c == ((r >> 5) & 3) * 128 + (r >> 7) * 32 + (r & 31))

        lane = iota((8, IJ), 1)
        pair = jnp.zeros((8, IJ), F32)
        for i in range(O):
            e = oe[i]
            pair = pair + jnp.where((lane >> 5) == i, e, 0.0) + jnp.where((lane & (O - 1)) == i, e, 0.0)
        row = iota((8, IJ), 0)
        base = -pair
        for b in range(8):
            base = base + jnp.where(row == b, ve[q * 8 + b], 0.0)
        for a in range(16):
            rden[8 * a : 8 * a + 8, :] = 1.0 / (base + ve[p * 16 + a])
        ab[...] = amp[...].reshape(ROWS, IJ).astype(BF16)

    prepare()
    pl.semaphore_wait(barrier, len(peers))

    def copy(src, dst, ss, rs, to):
        return pltpu.make_async_remote_copy(
            src_ref=src, dst_ref=dst, send_sem=ss, recv_sem=rs, device_id=to, device_id_type=MESH
        )

    def wait_bytes(ref, sem):
        pltpu.make_async_copy(ref, ref, sem).wait()

    for d in order:
        copy(blk, G.at[zh, zl, x, y, k], z_ss.at[d], z_rs.at[d], z_peer[d]).start()

    groups = [0]
    for d in range(1, 8):
        groups += [d, NZ - d]
    groups += [8]

    def first(n):
        e = groups[n]
        src_z = rot(z, NZ - e, NZ)
        h_, l_ = lax.div(src_z, NH), lax.rem(src_z, NH)
        if e:
            wait_bytes(blk, z_rs.at[e])
        piece = G.at[h_, l_, x, y, k]
        for to in x_peers if n % 2 == 0 else y_peers:
            copy(piece, piece, f_ss, f_rs.at[n], to).start()

    def second(n):
        e = groups[n]
        src_z = rot(z, NZ - e, NZ)
        h_, l_ = lax.div(src_z, NH), lax.rem(src_z, NH)
        wait_bytes(G.at[0, 0, 0:3, 0, 0], f_rs.at[n])
        if n % 2 == 0:
            piece, to_all = G.at[h_, l_, :, y, k], y_peers
        else:
            piece, to_all = G.at[h_, l_, x, :, k], x_peers
        for to in to_all:
            copy(piece, piece, s_ss, s_rs.at[n], to).start()

    def third(n):
        e = groups[n]
        src_z = rot(z, NZ - e, NZ)
        h_, l_ = lax.div(src_z, NH), lax.rem(src_z, NH)
        wait_bytes(G.at[0, 0, 0:3, :, 0], s_rs.at[n])
        piece = G.at[h_, l_, :, :, k]
        copy(piece, piece, c_ss, c_rs.at[n], sibling).start()

    for step in range(NZ + LAG2):
        if step < NZ:
            first(step)
        if 0 <= step - LAG1 < NZ:
            second(step - LAG1)
        if 0 <= step - LAG2 < NZ:
            third(step - LAG2)
    for n in range(NZ):
        wait_bytes(G.at[0, 0, :, :, 0], c_rs.at[n])

    @pl.loop(0, 8)
    def _(g):
        l_ = lax.div(g, 2)
        y0 = lax.rem(g, 2) * 2
        wide = jnp.concatenate(
            [G[:, l_, :, y0 + j // 2, j % 2].reshape(256, 128) for j in range(4)], axis=1
        )
        moved = dot(wide, shuf[...]).astype(BF16)
        for t in range(4):
            W[:, t, :, pl.ds(pl.multiple_of(g * 128, 128), 128)] = moved[
                :, 128 * t : 128 * t + 128
            ].reshape(16, 16, 128)

    def columns(n):
        return pl.ds(pl.multiple_of(n * COLS, COLS), COLS)

    def w_cols(n):
        return W[:, :, :, columns(n)].reshape(IJ, COLS)

    @pl.loop(0, IJ // COLS)
    def _(n):
        t1 = dot(ab[...], w_cols(n))
        tb[:, columns(n)] = t1.astype(BF16)
        d = drv[:, :, columns(n)].astype(F32).reshape(ROWS, COLS)
        b1 = (d + t1) * rden[:, columns(n)]
        high = b1.astype(BF16)
        lhs[0:ROWS, columns(n)] = high
        lhs[ROWS : 2 * ROWS, columns(n)] = (b1 - high.astype(F32)).astype(BF16)

    @pl.loop(0, IJ // COLS)
    def _(n):
        turned = dot(tb[...], perm[:, columns(n)]) * rden[:, columns(n)]
        lhs[2 * ROWS : 3 * ROWS, columns(n)] = turned.astype(BF16)

    @pl.loop(0, IJ // COLS)
    def _(n):
        both = dot(lhs[...], w_cols(n))
        x1[:, columns(n)] = both[0:ROWS] + both[ROWS : 2 * ROWS]
        x2b[:, columns(n)] = both[2 * ROWS :].astype(BF16)

    @pl.loop(0, IJ // COLS)
    def _(n):
        zz = x1[:, columns(n)] + dot(x2b[...], perm[:, columns(n)])
        d = drv[:, :, columns(n)].astype(F32).reshape(ROWS, COLS)
        x1[:, columns(n)] = d + zz
        zb = zz.astype(BF16)
        zsend[0, :, columns(n)] = zb[0:64]
        zsend[1, :, columns(n)] = zb[64:128]

    sends = []
    for h in range(2):
        to = (lax.div(q, 2), 2 * p + h)
        own = jnp.logical_and(to[0] == p, to[1] == q)
        sends.append((copy(zsend.at[h], zrecv.at[k], e_ss.at[h], e_rs.at[k], to), own))

        @pl.when(jnp.logical_not(own))
        def _():
            sends[h][0].start()

        @pl.when(own)
        def _():
            pltpu.make_async_copy(zsend.at[h], zrecv.at[k], e_rs.at[k]).start()

    for s in range(2):
        wait_bytes(zrecv.at[s], e_rs.at[s])

        @pl.loop(0, IJ // COLS)
        def _(n):
            turned = dot(zrecv[s], perm[:, columns(n)])
            for c in range(COLS // 128):
                vs[c] = turned[:, 128 * c : 128 * c + 128]
            for b in range(8):
                r = 8 * (8 * s + b)
                other = jnp.concatenate(
                    [vs[c, pl.ds(b, 8, stride=8), :] for c in range(COLS // 128)], axis=1
                )
                out[8 * s + b, :, columns(n)] = (
                    x1[r : r + 8, columns(n)] + other
                ) * rden[r : r + 8, columns(n)]

    for d in order:
        wait_bytes(blk, z_ss.at[d])
    wait_bytes(G.at[0:3, :, :, 0, 0], f_ss)
    wait_bytes(G.at[0:3, :, :, :, 0], s_ss)
    wait_bytes(G.at[:, :, :, :, 0], c_ss)
    for h in range(2):

        @pl.when(jnp.logical_not(sends[h][1]))
        def _():
            sends[h][0].wait_send()


def on_device(amplitudes, driving, ladder, block_mask, virt_energy, occ_energy):
    vmem = pl.BlockSpec(memory_space=pltpu.VMEM)
    smem = pl.BlockSpec(memory_space=pltpu.SMEM)
    dma = pltpu.SemaphoreType.DMA
    return pl.pallas_call(
        kernel,
        out_shape=jax.ShapeDtypeStruct(amplitudes.shape, F32),
        in_specs=[vmem, vmem, vmem, smem, smem, smem],
        out_specs=vmem,
        scratch_shapes=[
            pltpu.VMEM((NH, NH, NX, NX, 2, 16, 128), BF16),
            pltpu.VMEM((16, 4, 16, IJ), BF16),
            pltpu.VMEM((IJ, IJ), BF16),
            pltpu.VMEM((512, 512), BF16),
            pltpu.VMEM((16, 128), BF16),
            pltpu.VMEM((ROWS, IJ), F32),
            pltpu.VMEM((ROWS, IJ), BF16),
            pltpu.VMEM((ROWS, IJ), BF16),
            pltpu.VMEM((3 * ROWS, IJ), BF16),
            pltpu.VMEM((ROWS, IJ), F32),
            pltpu.VMEM((ROWS, IJ), BF16),
            pltpu.VMEM((2, 64, IJ), BF16),
            pltpu.VMEM((2, 64, IJ), BF16),
            pltpu.VMEM((COLS // 128, 64, 128), F32),
            dma((NZ,)),
            dma((NZ,)),
            dma(()),
            dma((NZ,)),
            dma(()),
            dma((NZ,)),
            dma(()),
            dma((NZ,)),
            dma((2,)),
            dma((2,)),
        ],
        compiler_params=pltpu.CompilerParams(collective_id=0, has_side_effects=True),
    )(amplitudes, driving, ladder, block_mask, virt_energy, occ_energy)


def solution(mesh):
    placed = (P("aa", "ba", None), P("aa", "ba", None), P("aa", "ba"), P(), P(), P())
    return jax.shard_map(
        on_device, mesh=mesh, in_specs=placed, out_specs=P("aa", "ba", None), check_vma=False
    )
```

```python
import jax
import jax.numpy as jnp
from jax import lax
from jax.experimental import pallas as pl
from jax.experimental.pallas import tpu as pltpu
from jax.sharding import PartitionSpec as P

MESH = pl.DeviceIdType.MESH
F32 = jnp.float32
BF16 = jnp.bfloat16
O = 32
NX = 4
NH = 4
NZ = 16
IJ = 1024
ROWS = 128
COLS = 256
CHUNKS = IJ // COLS
NEAR = (1, 15, 2, 14, 3, 13, 4, 12)
GROUPS = (0,) + NEAR + (5, 11, 6, 10, 7, 9, 8)
HOP, BASE = 0.78, 0.88


def arrival(e):
    d = min(e, NZ - e)
    if d == 0:
        return 0.0
    return BASE + HOP * d if d <= 4 else 2 * BASE + HOP * d


def plan():
    events = []
    for n, e in enumerate(GROUPS):
        t = arrival(e)
        events += [(t, 0, n), (t + 2.5, 1, n), (t + 5.0, 2, n), (t + 6.6, 3, n)]
    return [(kind, n) for _, kind, n in sorted(events)]


def iota(shape, dim):
    return lax.broadcasted_iota(jnp.int32, shape, dim)


def onehot(cond):
    return jnp.where(cond, 1.0, 0.0).astype(BF16)


def dot(a, b):
    return jnp.dot(a, b, preferred_element_type=F32)


def kernel(
    amp_hbm, drv_hbm, lad, mask, ve, oe, out,
    G, W, perm, shuf, blk, amp, drv, rden, ab, tacc, tb, lhs, x1, x2b, zsend, zrecv, vs,
    in_s, z_ss, z_rs, f_ss, f_rs, s_ss, s_rs, c_ss, c_rs, e_ss, e_rs,
):
    p = lax.axis_index("aa")
    q = lax.axis_index("ba")
    zh, x = lax.div(p, NX), lax.rem(p, NX)
    zl = lax.div(q, 2 * NX)
    y = lax.rem(lax.div(q, 2), NX)
    k = lax.rem(q, 2)
    z = zh * NH + zl

    def dev(z_, x_, y_, k_):
        return (lax.div(z_, NH) * NX + x_, lax.rem(z_, NH) * (2 * NX) + y_ * 2 + k_)

    def rot(v, d, n):
        return lax.rem(v + d, n)

    x_peers = [dev(z, rot(x, d, NX), y, k) for d in (2, 1, 3)]
    y_peers = [dev(z, x, rot(y, d, NX), k) for d in (2, 1, 3)]
    sibling = dev(z, x, y, 1 - k)
    z_peer = {d: dev(rot(z, d, NZ), x, y, k) for d in NEAR}

    barrier = pltpu.get_barrier_semaphore()
    peers = [z_peer[d] for d in reversed(NEAR)] + x_peers + y_peers + [sibling]
    for peer in peers:
        pl.semaphore_signal(barrier, inc=1, device_id=peer, device_id_type=MESH)

    loads = [
        pltpu.make_async_copy(amp_hbm, amp, in_s.at[0]),
        pltpu.make_async_copy(drv_hbm, drv, in_s.at[1]),
    ]
    for load in loads:
        load.start()

    keep = mask[p, lax.div(q, 2)].astype(F32)
    eye = onehot(iota((64, 64), 0) == iota((64, 64), 1))
    rows = lax.dot_general(
        eye, lad[...], (((1,), (1,)), ((), ())), preferred_element_type=F32
    ).astype(BF16)
    packed = jnp.zeros((16, 128), F32)
    for t in range(4):
        place = onehot(iota((32, 128), 1) == iota((32, 128), 0) + 32 * t)
        packed = packed + dot(rows[16 * t : 16 * t + 16, :], place)
    packed = (packed * keep).astype(BF16)
    blk[...] = packed
    G[zh, zl, k, x, y] = packed

    def copy(src, dst, ss, rs, to):
        return pltpu.make_async_remote_copy(
            src_ref=src, dst_ref=dst, send_sem=ss, recv_sem=rs, device_id=to, device_id_type=MESH
        )

    def wait_bytes(ref, sem):
        pltpu.make_async_copy(ref, ref, sem).wait()

    pl.semaphore_wait(barrier, len(peers))
    for d in reversed(NEAR):
        copy(blk, G.at[zh, zl, k, x, y], z_ss.at[d], z_rs.at[d], z_peer[d]).start()

    def plane(e):
        src_z = rot(z, NZ - e, NZ)
        return lax.div(src_z, NH), lax.rem(src_z, NH)

    def first(n):
        e = GROUPS[n]
        h_, l_ = plane(e)
        piece = G.at[h_, l_, k, x, y]
        if e:
            wait_bytes(blk, z_rs.at[e])
        if 1 <= e <= 4:
            copy(piece, piece, z_ss.at[e + 4], z_rs.at[e + 4], z_peer[4]).start()
        if 13 <= e <= 15:
            copy(piece, piece, z_ss.at[e - 4], z_rs.at[e - 4], z_peer[12]).start()
        for to in x_peers if n % 2 == 0 else y_peers:
            copy(piece, piece, f_ss, f_rs.at[n], to).start()

    def second(n):
        h_, l_ = plane(GROUPS[n])
        wait_bytes(G.at[0, 0, 0, 0, 0:3], f_rs.at[n])
        if n % 2 == 0:
            piece, to_all = G.at[h_, l_, k, :, y], y_peers
        else:
            piece, to_all = G.at[h_, l_, k, x], x_peers
        for to in to_all:
            copy(piece, piece, s_ss, s_rs.at[n], to).start()

    def third(n):
        h_, l_ = plane(GROUPS[n])
        wait_bytes(G.at[0, 0, 0, 0:3], s_rs.at[n])
        piece = G.at[h_, l_, k]
        copy(piece, piece, c_ss, c_rs.at[n], sibling).start()

    def use(n):
        h_, l_ = plane(GROUPS[n])
        wait_bytes(G.at[0, 0, 0], c_rs.at[n])
        wide = jnp.concatenate(
            [
                jnp.concatenate(
                    [G[h_, l_, j % 2, :, 2 * g + j // 2].reshape(64, 128) for j in range(4)], axis=1
                )
                for g in range(2)
            ],
            axis=0,
        )
        moved = dot(wide, shuf[...]).astype(BF16)
        cols = pl.ds(pl.multiple_of(l_ * COLS, COLS), COLS)
        for t in range(4):
            W[pl.ds(h_ * NX, NX), t, :, cols] = jnp.concatenate(
                [moved[64 * g : 64 * g + 64, 128 * t : 128 * t + 128] for g in range(2)], axis=1
            ).reshape(NX, 16, COLS)
        block = W[pl.ds(h_ * NX, NX), :, :, cols].reshape(COLS, COLS)
        tacc[:, cols] += dot(ab[:, pl.ds(pl.multiple_of(h_ * COLS, COLS), COLS)], block)

    def prepare():
        r = iota((512, 512), 0)
        c = iota((512, 512), 1)
        shuf[...] = onehot(c == ((r >> 5) & 3) * 128 + (r >> 7) * 32 + (r & 31))
        tacc[...] = jnp.zeros((ROWS, IJ), F32)
        loads[0].wait()
        ab[...] = amp[...].reshape(ROWS, IJ).astype(BF16)

        @pl.loop(0, 8)
        def _(i):
            r = iota((128, IJ), 0) + i * 128
            c = iota((128, IJ), 1)
            perm[pl.ds(pl.multiple_of(i * 128, 128), 128), :] = onehot(
                r == (c & (O - 1)) * O + (c >> 5)
            )

        lane = iota((8, IJ), 1)
        pair = jnp.zeros((8, IJ), F32)
        for i in range(O):
            e = oe[i]
            pair = pair + jnp.where((lane >> 5) == i, e, 0.0) + jnp.where((lane & (O - 1)) == i, e, 0.0)
        row = iota((8, IJ), 0)
        base = -pair
        for b in range(8):
            base = base + jnp.where(row == b, ve[q * 8 + b], 0.0)
        for a in range(16):
            rden[8 * a : 8 * a + 8, :] = 1.0 / (base + ve[p * 16 + a])
        loads[1].wait()

    steps = [first, second, third, use]
    for i, (kind, n) in enumerate(plan()):
        if i == 1:
            prepare()
        steps[kind](n)

    def columns(n):
        return pl.ds(pl.multiple_of(n * COLS, COLS), COLS)

    def w_cols(n):
        return W[:, :, :, columns(n)].reshape(IJ, COLS)

    def wide_driving(n):
        return drv[:, :, columns(n)].astype(F32).reshape(ROWS, COLS)

    @pl.loop(0, CHUNKS)
    def _(n):
        t1 = tacc[:, columns(n)]
        tb[:, columns(n)] = t1.astype(BF16)
        b1 = (wide_driving(n) + t1) * rden[:, columns(n)]
        high = b1.astype(BF16)
        lhs[0:ROWS, columns(n)] = high
        lhs[ROWS : 2 * ROWS, columns(n)] = (b1 - high.astype(F32)).astype(BF16)

    @pl.loop(0, CHUNKS)
    def _(n):
        turned = dot(tb[...], perm[:, columns(n)]) * rden[:, columns(n)]
        lhs[2 * ROWS : 3 * ROWS, columns(n)] = turned.astype(BF16)

    @pl.loop(0, CHUNKS)
    def _(n):
        both = dot(lhs[...], w_cols(n))
        x1[:, columns(n)] = both[0:ROWS] + both[ROWS : 2 * ROWS]
        x2b[:, columns(n)] = both[2 * ROWS :].astype(BF16)

    def to_half(h):
        to = (lax.div(q, 2), 2 * p + h)
        return to, jnp.logical_and(to[0] == p, to[1] == q)

    def exchange(n, h):
        to, own = to_half(h)
        return copy(zsend.at[n, h], zrecv.at[n, k], e_ss.at[n, h], e_rs.at[n, k], to), own

    for n in range(CHUNKS):
        cols = slice(n * COLS, (n + 1) * COLS)
        zz = x1[:, cols] + dot(x2b[...], perm[:, cols])
        x1[:, cols] = drv[:, :, cols].astype(F32).reshape(ROWS, COLS) + zz
        zsend[n] = zz.astype(BF16).reshape(2, 64, COLS)
        for h in range(2):
            send, own = exchange(n, h)

            @pl.when(jnp.logical_not(own))
            def _():
                send.start()

            @pl.when(own)
            def _():
                pltpu.make_async_copy(zsend.at[n, h], zrecv.at[n, k], e_rs.at[n, k]).start()

    for n in range(CHUNKS):
        for s in range(2):
            wait_bytes(zrecv.at[n, s], e_rs.at[n, s])
        got = zrecv[n].reshape(ROWS, COLS)
        for m in range(CHUNKS):
            turned = dot(got, perm[n * COLS : (n + 1) * COLS, m * COLS : (m + 1) * COLS])
            for c in range(COLS // 128):
                part = turned[:, 128 * c : 128 * c + 128]
                if n:
                    vs[m * (COLS // 128) + c] += part
                else:
                    vs[m * (COLS // 128) + c] = part

    @pl.loop(0, IJ // 128)
    def _(c):
        cols = pl.ds(pl.multiple_of(c * 128, 128), 128)
        for s in range(2):
            for b in range(8):
                r = 8 * (8 * s + b)
                other = vs[c, pl.ds(64 * s + b, 8, stride=8), :]
                out[8 * s + b, :, cols] = (x1[r : r + 8, cols] + other) * rden[r : r + 8, cols]

    for d in NEAR + GROUPS[9:]:
        wait_bytes(blk, z_ss.at[d])
    wait_bytes(G.at[0:3, :, 0, :, 0], f_ss)
    wait_bytes(G.at[0:3, :, 0], s_ss)
    wait_bytes(G.at[:, :, 0], c_ss)
    for n in range(CHUNKS):
        for h in range(2):
            send, own = exchange(n, h)

            @pl.when(jnp.logical_not(own))
            def _():
                send.wait_send()


def on_device(amplitudes, driving, ladder, block_mask, virt_energy, occ_energy):
    vmem = pl.BlockSpec(memory_space=pltpu.VMEM)
    smem = pl.BlockSpec(memory_space=pltpu.SMEM)
    hbm = pl.BlockSpec(memory_space=pltpu.HBM)
    dma = pltpu.SemaphoreType.DMA
    return pl.pallas_call(
        kernel,
        out_shape=jax.ShapeDtypeStruct(amplitudes.shape, F32),
        in_specs=[hbm, hbm, vmem, smem, smem, smem],
        out_specs=vmem,
        scratch_shapes=[
            pltpu.VMEM((NH, NH, 2, NX, NX, 16, 128), BF16),
            pltpu.VMEM((16, 4, 16, IJ), BF16),
            pltpu.VMEM((IJ, IJ), BF16),
            pltpu.VMEM((512, 512), BF16),
            pltpu.VMEM((16, 128), BF16),
            pltpu.VMEM(amplitudes.shape, F32),
            pltpu.VMEM(driving.shape, BF16),
            pltpu.VMEM((ROWS, IJ), F32),
            pltpu.VMEM((ROWS, IJ), BF16),
            pltpu.VMEM((ROWS, IJ), F32),
            pltpu.VMEM((ROWS, IJ), BF16),
            pltpu.VMEM((3 * ROWS, IJ), BF16),
            pltpu.VMEM((ROWS, IJ), F32),
            pltpu.VMEM((ROWS, IJ), BF16),
            pltpu.VMEM((CHUNKS, 2, 64, COLS), BF16),
            pltpu.VMEM((CHUNKS, 2, 64, COLS), BF16),
            pltpu.VMEM((IJ // 128, ROWS, 128), F32),
            dma((2,)),
            dma((NZ,)),
            dma((NZ,)),
            dma(()),
            dma((NZ,)),
            dma(()),
            dma((NZ,)),
            dma(()),
            dma((NZ,)),
            dma((CHUNKS, 2)),
            dma((CHUNKS, 2)),
        ],
        compiler_params=pltpu.CompilerParams(collective_id=0, has_side_effects=True),
    )(amplitudes, driving, ladder.T, block_mask, virt_energy, occ_energy)


def solution(mesh):
    placed = (P("aa", "ba", None), P("aa", "ba", None), P("aa", "ba"), P(), P(), P())
    return jax.shard_map(
        on_device, mesh=mesh, in_specs=placed, out_specs=P("aa", "ba", None), check_vma=False
    )
```

```python
import jax
import jax.numpy as jnp
from jax import lax
from jax.experimental import pallas as pl
from jax.experimental.pallas import tpu as pltpu
from jax.sharding import PartitionSpec as P

MESH = pl.DeviceIdType.MESH
F32 = jnp.float32
BF16 = jnp.bfloat16
O = 32
NX = 4
NH = 4
NZ = 16
IJ = 1024
ROWS = 128
COLS = 256
CHUNKS = IJ // COLS
NEAR = (1, 15, 2, 14, 3, 13, 4, 12)
GROUPS = (0,) + NEAR + (5, 11, 6, 10, 7, 9, 8)
EARLY = 3
EROWS = 2 * EARLY * 8
LAG = 4
RAW_AT = 0


def plan():
    events = [(0, n) for n in range(NZ)] + [(1, n) for n in range(NZ)]
    for n in range(NZ + LAG):
        if n == RAW_AT:
            events.append((4, 0))
        if n < NZ:
            events.append((2, n))
        if n >= LAG:
            events.append((3, n - LAG))
    return events


def iota(shape, dim):
    return lax.broadcasted_iota(jnp.int32, shape, dim)


def onehot(cond):
    return jnp.where(cond, 1.0, 0.0).astype(BF16)


def dot(a, b):
    return jnp.dot(a, b, preferred_element_type=F32)


def kernel(
    amp_hbm, drv_hbm, lad, mask, ve, oe, out,
    G, W, perm, shuf, blk, amp, drv, abt, rden, ab, tb, lhs, x1, x2b, zsend, zrecv, vs,
    araw, draw, rden2, ab2, tb2, lhs2, x12, x2b2, in_s, r_ss, r_rs, z_ss, z_rs, f_ss, f_rs, s_ss, s_rs, c_ss, c_rs, e_ss, e_rs,
):
    p = lax.axis_index("aa")
    q = lax.axis_index("ba")
    zh, x = lax.div(p, NX), lax.rem(p, NX)
    zl = lax.div(q, 2 * NX)
    y = lax.rem(lax.div(q, 2), NX)
    k = lax.rem(q, 2)
    z = zh * NH + zl

    def dev(z_, x_, y_, k_):
        return (lax.div(z_, NH) * NX + x_, lax.rem(z_, NH) * (2 * NX) + y_ * 2 + k_)

    def rot(v, d, n):
        return lax.rem(v + d, n)

    x_peers = [dev(z, rot(x, d, NX), y, k) for d in (2, 1, 3)]
    y_peers = [dev(z, x, rot(y, d, NX), k) for d in (2, 1, 3)]
    sibling = dev(z, x, y, 1 - k)
    z_peer = {d: dev(rot(z, d, NZ), x, y, k) for d in NEAR}

    barrier = pltpu.get_barrier_semaphore()
    peers = [z_peer[d] for d in reversed(NEAR)] + x_peers + y_peers + [sibling]
    peers += [dev(z, rot(x, d, NX), y, 1 - k) for d in (2, 1, 3)]
    peers += [dev(z, x, rot(y, d, NX), 1 - k) for d in (2, 1, 3)]
    for peer in peers:
        pl.semaphore_signal(barrier, inc=1, device_id=peer, device_id_type=MESH)

    loads = [
        pltpu.make_async_copy(amp_hbm, amp, in_s.at[0]),
        pltpu.make_async_copy(drv_hbm, drv, in_s.at[1]),
    ]
    for load in loads:
        load.start()

    keep = mask[p, lax.div(q, 2)].astype(F32)
    eye = onehot(iota((64, 64), 0) == iota((64, 64), 1))
    rows = lax.dot_general(
        eye, lad[...], (((1,), (1,)), ((), ())), preferred_element_type=F32
    ).astype(BF16)
    packed = jnp.zeros((16, 128), F32)
    for t in range(4):
        place = onehot(iota((32, 128), 1) == iota((32, 128), 0) + 32 * t)
        packed = packed + dot(rows[16 * t : 16 * t + 16, :], place)
    packed = (packed * keep).astype(BF16)
    blk[...] = packed
    G[zh, zl, k, x, y] = packed

    def copy(src, dst, ss, rs, to):
        return pltpu.make_async_remote_copy(
            src_ref=src, dst_ref=dst, send_sem=ss, recv_sem=rs, device_id=to, device_id_type=MESH
        )

    def wait_bytes(ref, sem):
        pltpu.make_async_copy(ref, ref, sem).wait()

    pl.semaphore_wait(barrier, len(peers))
    for d in reversed(NEAR):
        copy(blk, G.at[zh, zl, k, x, y], z_ss.at[d], z_rs.at[d], z_peer[d]).start()

    def plane(e):
        src_z = rot(z, NZ - e, NZ)
        return lax.div(src_z, NH), lax.rem(src_z, NH)

    def first(n):
        e = GROUPS[n]
        h_, l_ = plane(e)
        piece = G.at[h_, l_, k, x, y]
        if e:
            wait_bytes(blk, z_rs.at[e])
        if 1 <= e <= 4:
            copy(piece, piece, z_ss.at[e + 4], z_rs.at[e + 4], z_peer[4]).start()
        if 13 <= e <= 15:
            copy(piece, piece, z_ss.at[e - 4], z_rs.at[e - 4], z_peer[12]).start()
        for to in x_peers if n % 2 == 0 else y_peers:
            copy(piece, piece, f_ss, f_rs.at[n], to).start()

    def second(n):
        h_, l_ = plane(GROUPS[n])
        wait_bytes(G.at[0, 0, 0, 0, 0:3], f_rs.at[n])
        if n % 2 == 0:
            piece, to_all = G.at[h_, l_, k, :, y], y_peers
        else:
            piece, to_all = G.at[h_, l_, k, x], x_peers
        for to in to_all:
            copy(piece, piece, s_ss, s_rs.at[n], to).start()

    def third(n):
        h_, l_ = plane(GROUPS[n])
        wait_bytes(G.at[0, 0, 0, 0:3], s_rs.at[n])
        piece = G.at[h_, l_, k]
        copy(piece, piece, c_ss, c_rs.at[n], sibling).start()

    def use(n):
        h_, l_ = plane(GROUPS[n])
        wait_bytes(G.at[0, 0, 0], c_rs.at[n])
        wide = jnp.concatenate(
            [
                jnp.concatenate(
                    [G[h_, l_, j % 2, :, 2 * g + j // 2].reshape(64, 128) for j in range(4)], axis=1
                )
                for g in range(2)
            ],
            axis=0,
        )
        moved = dot(wide, shuf[...]).astype(BF16)
        cols = pl.ds(pl.multiple_of(l_ * COLS, COLS), COLS)
        for t in range(4):
            W[pl.ds(h_ * NX, NX), t, :, cols] = jnp.concatenate(
                [moved[64 * g : 64 * g + 64, 128 * t : 128 * t + 128] for g in range(2)], axis=1
            ).reshape(NX, 16, COLS)

    def prepare():
        r = iota((512, 512), 0)
        c = iota((512, 512), 1)
        shuf[...] = onehot(c == ((r >> 5) & 3) * 128 + (r >> 7) * 32 + (r & 31))
        loads[0].wait()
        ab[...] = amp[...].reshape(ROWS, IJ).astype(BF16)
        abt[...] = amp[...].astype(BF16)

        @pl.loop(0, 8)
        def _(i):
            r = iota((128, IJ), 0) + i * 128
            c = iota((128, IJ), 1)
            perm[pl.ds(pl.multiple_of(i * 128, 128), 128), :] = onehot(
                r == (c & (O - 1)) * O + (c >> 5)
            )

        lane = iota((8, IJ), 1)
        pair = jnp.zeros((8, IJ), F32)
        for i in range(O):
            e = oe[i]
            pair = pair + jnp.where((lane >> 5) == i, e, 0.0) + jnp.where((lane & (O - 1)) == i, e, 0.0)
        row = iota((8, IJ), 0)

        def over(first_b):
            base = -pair
            for b in range(8):
                base = base + jnp.where(row == b, ve[first_b + b], 0.0)
            return base

        base = over(q * 8)
        for a in range(16):
            rden[8 * a : 8 * a + 8, :] = 1.0 / (base + ve[p * 16 + a])
        for s in range(2):
            base = over(p * 16 + 8 * s)
            for a in range(EARLY):
                r = 8 * (s * EARLY + a)
                rden2[r : r + 8, :] = 1.0 / (base + ve[q * 8 + a])
        loads[1].wait()

    def give(src, dst, ss, rs, h):
        to = (lax.div(q, 2), 2 * p + h)
        own = jnp.logical_and(to[0] == p, to[1] == q)
        send = copy(src, dst, ss, rs, to)

        @pl.when(jnp.logical_not(own))
        def _():
            send.start()

        @pl.when(own)
        def _():
            pltpu.make_async_copy(src, dst, rs).start()

        def done():
            @pl.when(jnp.logical_not(own))
            def _():
                send.wait_send()

        return done

    given = []

    def early(_):
        for h in range(2):
            for j, (src, dst) in enumerate(((abt, araw), (drv, draw))):
                piece = src.at[8 * h : 8 * h + EARLY]
                given.append(give(piece, dst.at[k], r_ss.at[h, j], r_rs.at[k, j], h))

    steps = [first, second, third, use, early]
    for i, (kind, n) in enumerate(plan()):
        if i == 1:
            prepare()
        steps[kind](n)

    def columns(n):
        return pl.ds(pl.multiple_of(n * COLS, COLS), COLS)

    def w_cols(n):
        return W[:, :, :, columns(n)].reshape(IJ, COLS)

    def halves(count, tile, drive, over_den, t_, l_, one, two):
        @pl.loop(0, CHUNKS)
        def _(n):
            t1 = dot(tile[...], w_cols(n))
            t_[:, columns(n)] = t1.astype(BF16)
            b1 = (drive(n) + t1) * over_den[:, columns(n)]
            high = b1.astype(BF16)
            l_[0:count, columns(n)] = high
            l_[count : 2 * count, columns(n)] = (b1 - high.astype(F32)).astype(BF16)

        @pl.loop(0, CHUNKS)
        def _(n):
            turned = dot(t_[...], perm[:, columns(n)]) * over_den[:, columns(n)]
            l_[2 * count : 3 * count, columns(n)] = turned.astype(BF16)

        @pl.loop(0, CHUNKS)
        def _(n):
            both = dot(l_[...], w_cols(n))
            one[:, columns(n)] = both[0:count] + both[count : 2 * count]
            two[:, columns(n)] = both[2 * count :].astype(BF16)

    def drive(n):
        return drv[:, :, columns(n)].astype(F32).reshape(ROWS, COLS)

    halves(ROWS, ab, drive, rden, tb, lhs, x1, x2b)

    for n in range(CHUNKS):
        cols = slice(n * COLS, (n + 1) * COLS)
        zz = x1[:, cols] + dot(x2b[...], perm[:, cols])
        x1[:, cols] = drv[:, :, cols].astype(F32).reshape(ROWS, COLS) + zz
        zsend[n] = zz.reshape(2, 8, 8, COLS).astype(BF16)
        for h in range(2):
            given.append(
                give(
                    zsend.at[n, h, EARLY:8], zrecv.at[n, k, EARLY:8], e_ss.at[n, h], e_rs.at[n, k], h
                )
            )

    for s in range(2):
        for j, dst in enumerate((araw, draw)):
            wait_bytes(dst.at[s], r_rs.at[s, j])
    ab2[...] = araw[...].astype(F32).reshape(EROWS, IJ).astype(BF16)

    def early_drive(n):
        return draw[:, :, :, columns(n)].astype(F32).reshape(EROWS, COLS)

    halves(EROWS, ab2, early_drive, rden2, tb2, lhs2, x12, x2b2)
    for n in range(CHUNKS):
        cols = slice(n * COLS, (n + 1) * COLS)
        zz = x12[:, cols] + dot(x2b2[...], perm[:, cols])
        zrecv[n, :, 0:EARLY] = zz.reshape(2, EARLY, 8, COLS).astype(BF16)

    for n in range(CHUNKS):
        for s in range(2):
            wait_bytes(zrecv.at[n, s, EARLY:8], e_rs.at[n, s])
        got = zrecv[n].astype(F32).reshape(ROWS, COLS).astype(BF16)
        for m in range(CHUNKS):
            turned = dot(got, perm[n * COLS : (n + 1) * COLS, m * COLS : (m + 1) * COLS])
            for c in range(COLS // 128):
                part = turned[:, 128 * c : 128 * c + 128]
                if n:
                    vs[m * (COLS // 128) + c] += part
                else:
                    vs[m * (COLS // 128) + c] = part

    @pl.loop(0, IJ // 128)
    def _(c):
        cols = pl.ds(pl.multiple_of(c * 128, 128), 128)
        for s in range(2):
            for b in range(8):
                r = 8 * (8 * s + b)
                other = vs[c, pl.ds(64 * s + b, 8, stride=8), :]
                out[8 * s + b, :, cols] = (x1[r : r + 8, cols] + other) * rden[r : r + 8, cols]

    for d in NEAR + GROUPS[9:]:
        wait_bytes(blk, z_ss.at[d])
    wait_bytes(G.at[0:3, :, 0, :, 0], f_ss)
    wait_bytes(G.at[0:3, :, 0], s_ss)
    wait_bytes(G.at[:, :, 0], c_ss)
    for done in given:
        done()


def on_device(amplitudes, driving, ladder, block_mask, virt_energy, occ_energy):
    vmem = pl.BlockSpec(memory_space=pltpu.VMEM)
    smem = pl.BlockSpec(memory_space=pltpu.SMEM)
    hbm = pl.BlockSpec(memory_space=pltpu.HBM)
    dma = pltpu.SemaphoreType.DMA
    return pl.pallas_call(
        kernel,
        out_shape=jax.ShapeDtypeStruct(amplitudes.shape, F32),
        in_specs=[hbm, hbm, vmem, smem, smem, smem],
        out_specs=vmem,
        scratch_shapes=[
            pltpu.VMEM((NH, NH, 2, NX, NX, 16, 128), BF16),
            pltpu.VMEM((16, 4, 16, IJ), BF16),
            pltpu.VMEM((IJ, IJ), BF16),
            pltpu.VMEM((512, 512), BF16),
            pltpu.VMEM((16, 128), BF16),
            pltpu.VMEM(amplitudes.shape, F32),
            pltpu.VMEM(driving.shape, BF16),
            pltpu.VMEM(amplitudes.shape, BF16),
            pltpu.VMEM((ROWS, IJ), F32),
            pltpu.VMEM((ROWS, IJ), BF16),
            pltpu.VMEM((ROWS, IJ), BF16),
            pltpu.VMEM((3 * ROWS, IJ), BF16),
            pltpu.VMEM((ROWS, IJ), F32),
            pltpu.VMEM((ROWS, IJ), BF16),
            pltpu.VMEM((CHUNKS, 2, 8, 8, COLS), BF16),
            pltpu.VMEM((CHUNKS, 2, 8, 8, COLS), BF16),
            pltpu.VMEM((IJ // 128, ROWS, 128), F32),
            pltpu.VMEM((2, EARLY, 8, IJ), BF16),
            pltpu.VMEM((2, EARLY, 8, IJ), BF16),
            pltpu.VMEM((EROWS, IJ), F32),
            pltpu.VMEM((EROWS, IJ), BF16),
            pltpu.VMEM((EROWS, IJ), BF16),
            pltpu.VMEM((3 * EROWS, IJ), BF16),
            pltpu.VMEM((EROWS, IJ), F32),
            pltpu.VMEM((EROWS, IJ), BF16),
            dma((2,)),
            dma((2, 2)),
            dma((2, 2)),
            dma((NZ,)),
            dma((NZ,)),
            dma(()),
            dma((NZ,)),
            dma(()),
            dma((NZ,)),
            dma(()),
            dma((NZ,)),
            dma((CHUNKS, 2)),
            dma((CHUNKS, 2)),
        ],
        compiler_params=pltpu.CompilerParams(collective_id=0, has_side_effects=True),
    )(amplitudes, driving, ladder.T, block_mask, virt_energy, occ_energy)


def solution(mesh):
    placed = (P("aa", "ba", None), P("aa", "ba", None), P("aa", "ba"), P(), P(), P())
    return jax.shard_map(
        on_device, mesh=mesh, in_specs=placed, out_specs=P("aa", "ba", None), check_vma=False
    )
```

```python
import jax
import jax.numpy as jnp
from jax import lax
from jax.experimental import pallas as pl
from jax.experimental.pallas import tpu as pltpu
from jax.sharding import PartitionSpec as P

MESH = pl.DeviceIdType.MESH
F32 = jnp.float32
BF16 = jnp.bfloat16
O = 32
NX = 4
NH = 4
NZ = 16
IJ = 1024
ROWS = 128
COLS = 256
CHUNKS = IJ // COLS
NEAR = (1, 15, 2, 14, 3, 13, 4, 12)
GROUPS = (0,) + NEAR + (5, 11, 6, 10, 7, 9, 8)
EARLY = 3
EROWS = 2 * EARLY * 8
LAG = 4
RAW_AT = 0


def plan():
    events = [(0, n) for n in range(NZ)] + [(1, n) for n in range(NZ)]
    for n in range(NZ + LAG):
        if n == RAW_AT:
            events.append((4, 0))
        if n < NZ:
            events.append((2, n))
        if n >= LAG:
            events.append((3, n - LAG))
    return events


def iota(shape, dim):
    return lax.broadcasted_iota(jnp.int32, shape, dim)


def onehot(cond):
    return jnp.where(cond, 1.0, 0.0).astype(BF16)


def dot(a, b):
    return jnp.dot(a, b, preferred_element_type=F32)


def kernel(
    amp_hbm, drv_hbm, lad, mask, ve, oe, out,
    G, W, perm, shuf, blk, amp, drv, abt, rden, ab, tb, lhs, cb, x1, x2b, zsend, zrecv, vs,
    araw, draw, rden2, ab2, tb2, lhs2, cb2, x2b2, in_s, r_ss, r_rs, z_ss, z_rs, f_ss, f_rs, s_ss, s_rs, c_ss, c_rs, e_ss, e_rs,
):
    p = lax.axis_index("aa")
    q = lax.axis_index("ba")
    zh, x = lax.div(p, NX), lax.rem(p, NX)
    zl = lax.div(q, 2 * NX)
    y = lax.rem(lax.div(q, 2), NX)
    k = lax.rem(q, 2)
    z = zh * NH + zl

    def dev(z_, x_, y_, k_):
        return (lax.div(z_, NH) * NX + x_, lax.rem(z_, NH) * (2 * NX) + y_ * 2 + k_)

    def rot(v, d, n):
        return lax.rem(v + d, n)

    x_peers = [dev(z, rot(x, d, NX), y, k) for d in (2, 1, 3)]
    y_peers = [dev(z, x, rot(y, d, NX), k) for d in (2, 1, 3)]
    sibling = dev(z, x, y, 1 - k)
    z_peer = {d: dev(rot(z, d, NZ), x, y, k) for d in NEAR}

    barrier = pltpu.get_barrier_semaphore()
    peers = [z_peer[d] for d in reversed(NEAR)] + x_peers + y_peers + [sibling]
    peers += [dev(z, rot(x, d, NX), y, 1 - k) for d in (2, 1, 3)]
    peers += [dev(z, x, rot(y, d, NX), 1 - k) for d in (2, 1, 3)]
    for peer in peers:
        pl.semaphore_signal(barrier, inc=1, device_id=peer, device_id_type=MESH)

    loads = [
        pltpu.make_async_copy(amp_hbm, amp, in_s.at[0]),
        pltpu.make_async_copy(drv_hbm, drv, in_s.at[1]),
    ]
    for load in loads:
        load.start()

    keep = mask[p, lax.div(q, 2)].astype(F32)
    eye = onehot(iota((64, 64), 0) == iota((64, 64), 1))
    rows = lax.dot_general(
        eye, lad[...], (((1,), (1,)), ((), ())), preferred_element_type=F32
    ).astype(BF16)
    packed = jnp.zeros((16, 128), F32)
    for t in range(4):
        place = onehot(iota((32, 128), 1) == iota((32, 128), 0) + 32 * t)
        packed = packed + dot(rows[16 * t : 16 * t + 16, :], place)
    packed = (packed * keep).astype(BF16)
    blk[...] = packed
    G[zh, zl, k, x, y] = packed

    def copy(src, dst, ss, rs, to):
        return pltpu.make_async_remote_copy(
            src_ref=src, dst_ref=dst, send_sem=ss, recv_sem=rs, device_id=to, device_id_type=MESH
        )

    def wait_bytes(ref, sem):
        pltpu.make_async_copy(ref, ref, sem).wait()

    pl.semaphore_wait(barrier, len(peers))
    for d in reversed(NEAR):
        copy(blk, G.at[zh, zl, k, x, y], z_ss.at[d], z_rs.at[d], z_peer[d]).start()

    def plane(e):
        src_z = rot(z, NZ - e, NZ)
        return lax.div(src_z, NH), lax.rem(src_z, NH)

    def first(n):
        e = GROUPS[n]
        h_, l_ = plane(e)
        piece = G.at[h_, l_, k, x, y]
        if e:
            wait_bytes(blk, z_rs.at[e])
        if 1 <= e <= 4:
            copy(piece, piece, z_ss.at[e + 4], z_rs.at[e + 4], z_peer[4]).start()
        if 13 <= e <= 15:
            copy(piece, piece, z_ss.at[e - 4], z_rs.at[e - 4], z_peer[12]).start()
        for to in x_peers if n % 2 == 0 else y_peers:
            copy(piece, piece, f_ss, f_rs.at[n], to).start()

    def second(n):
        h_, l_ = plane(GROUPS[n])
        wait_bytes(G.at[0, 0, 0, 0, 0:3], f_rs.at[n])
        if n % 2 == 0:
            piece, to_all = G.at[h_, l_, k, :, y], y_peers
        else:
            piece, to_all = G.at[h_, l_, k, x], x_peers
        for to in to_all:
            copy(piece, piece, s_ss, s_rs.at[n], to).start()

    def third(n):
        h_, l_ = plane(GROUPS[n])
        wait_bytes(G.at[0, 0, 0, 0:3], s_rs.at[n])
        piece = G.at[h_, l_, k]
        copy(piece, piece, c_ss, c_rs.at[n], sibling).start()

    def use(n):
        h_, l_ = plane(GROUPS[n])
        wait_bytes(G.at[0, 0, 0], c_rs.at[n])
        wide = jnp.concatenate(
            [
                jnp.concatenate(
                    [G[h_, l_, j % 2, :, 2 * g + j // 2].reshape(64, 128) for j in range(4)], axis=1
                )
                for g in range(2)
            ],
            axis=0,
        )
        moved = dot(wide, shuf[...]).astype(BF16)
        cols = pl.ds(pl.multiple_of(l_ * COLS, COLS), COLS)
        for t in range(4):
            W[pl.ds(h_ * NX, NX), t, :, cols] = jnp.concatenate(
                [moved[64 * g : 64 * g + 64, 128 * t : 128 * t + 128] for g in range(2)], axis=1
            ).reshape(NX, 16, COLS)

    def prepare():
        r = iota((512, 512), 0)
        c = iota((512, 512), 1)
        shuf[...] = onehot(c == ((r >> 5) & 3) * 128 + (r >> 7) * 32 + (r & 31))
        loads[0].wait()
        ab[...] = amp[...].reshape(ROWS, IJ).astype(BF16)
        abt[...] = amp[...].astype(BF16)

        @pl.loop(0, 8)
        def _(i):
            r = iota((128, IJ), 0) + i * 128
            c = iota((128, IJ), 1)
            perm[pl.ds(pl.multiple_of(i * 128, 128), 128), :] = onehot(
                r == (c & (O - 1)) * O + (c >> 5)
            )

        lane = iota((8, IJ), 1)
        pair = jnp.zeros((8, IJ), F32)
        for i in range(O):
            e = oe[i]
            pair = pair + jnp.where((lane >> 5) == i, e, 0.0) + jnp.where((lane & (O - 1)) == i, e, 0.0)
        row = iota((8, IJ), 0)

        def over(first_b):
            base = -pair
            for b in range(8):
                base = base + jnp.where(row == b, ve[first_b + b], 0.0)
            return base

        base = over(q * 8)
        for a in range(16):
            rden[8 * a : 8 * a + 8, :] = 1.0 / (base + ve[p * 16 + a])
        for s in range(2):
            base = over(p * 16 + 8 * s)
            for a in range(EARLY):
                r = 8 * (s * EARLY + a)
                rden2[r : r + 8, :] = 1.0 / (base + ve[q * 8 + a])
        loads[1].wait()

    def give(src, dst, ss, rs, h):
        to = (lax.div(q, 2), 2 * p + h)
        own = jnp.logical_and(to[0] == p, to[1] == q)
        send = copy(src, dst, ss, rs, to)

        @pl.when(jnp.logical_not(own))
        def _():
            send.start()

        @pl.when(own)
        def _():
            pltpu.make_async_copy(src, dst, rs).start()

        def done():
            @pl.when(jnp.logical_not(own))
            def _():
                send.wait_send()

        return done

    given = []

    def early(_):
        for h in range(2):
            for j, (src, dst) in enumerate(((abt, araw), (drv, draw))):
                piece = src.at[8 * h : 8 * h + EARLY]
                given.append(give(piece, dst.at[k], r_ss.at[h, j], r_rs.at[k, j], h))

    steps = [first, second, third, use, early]
    for i, (kind, n) in enumerate(plan()):
        if i == 1:
            prepare()
        steps[kind](n)

    def columns(n):
        if isinstance(n, int):
            return slice(n * COLS, (n + 1) * COLS)
        return pl.ds(pl.multiple_of(n * COLS, COLS), COLS)

    def w_cols(n):
        return W[:, :, :, columns(n)].reshape(IJ, COLS)

    def halves(count, tile, drive, over_den, t_, b_, c_, two):
        @pl.loop(0, CHUNKS)
        def _(n):
            t1 = dot(tile[...], w_cols(n))
            t_[:, columns(n)] = t1.astype(BF16)
            b1 = (drive(n) + t1) * over_den[:, columns(n)]
            high = b1.astype(BF16)
            b_[0:count, columns(n)] = high
            b_[count : 2 * count, columns(n)] = (b1 - high.astype(F32)).astype(BF16)

        @pl.loop(0, CHUNKS)
        def _(n):
            turned = dot(t_[...], perm[:, columns(n)]) * over_den[:, columns(n)]
            c_[:, columns(n)] = turned.astype(BF16)

        @pl.loop(0, CHUNKS)
        def _(n):
            two[:, columns(n)] = dot(c_[...], w_cols(n)).astype(BF16)

    def joined(n, count, b_, two):
        both = dot(b_[...], w_cols(n))
        return both[0:count] + both[count : 2 * count] + dot(two[...], perm[:, columns(n)])

    def drive(n):
        return drv[:, :, columns(n)].astype(F32).reshape(ROWS, COLS)

    halves(ROWS, ab, drive, rden, tb, lhs, cb, x2b)

    for n in range(CHUNKS):
        cols = slice(n * COLS, (n + 1) * COLS)
        zz = joined(n, ROWS, lhs, x2b)
        x1[:, cols] = drv[:, :, cols].astype(F32).reshape(ROWS, COLS) + zz
        zsend[n] = zz.reshape(2, 8, 8, COLS).astype(BF16)
        for h in range(2):
            given.append(
                give(
                    zsend.at[n, h, EARLY:8], zrecv.at[n, k, EARLY:8], e_ss.at[n, h], e_rs.at[n, k], h
                )
            )

    for s in range(2):
        for j, dst in enumerate((araw, draw)):
            wait_bytes(dst.at[s], r_rs.at[s, j])
    ab2[...] = araw[...].astype(F32).reshape(EROWS, IJ).astype(BF16)

    def early_drive(n):
        return draw[:, :, :, columns(n)].astype(F32).reshape(EROWS, COLS)

    halves(EROWS, ab2, early_drive, rden2, tb2, lhs2, cb2, x2b2)
    for n in range(CHUNKS):
        zz = joined(n, EROWS, lhs2, x2b2)
        zrecv[n, :, 0:EARLY] = zz.reshape(2, EARLY, 8, COLS).astype(BF16)

    for n in range(CHUNKS):
        for s in range(2):
            wait_bytes(zrecv.at[n, s, EARLY:8], e_rs.at[n, s])
        got = zrecv[n].astype(F32).reshape(ROWS, COLS).astype(BF16)
        for m in range(CHUNKS):
            turned = dot(got, perm[n * COLS : (n + 1) * COLS, m * COLS : (m + 1) * COLS])
            for c in range(COLS // 128):
                part = turned[:, 128 * c : 128 * c + 128]
                if n:
                    vs[m * (COLS // 128) + c] += part
                else:
                    vs[m * (COLS // 128) + c] = part

    @pl.loop(0, IJ // 128)
    def _(c):
        cols = pl.ds(pl.multiple_of(c * 128, 128), 128)
        for s in range(2):
            for b in range(8):
                r = 8 * (8 * s + b)
                other = vs[c, pl.ds(64 * s + b, 8, stride=8), :]
                out[8 * s + b, :, cols] = (x1[r : r + 8, cols] + other) * rden[r : r + 8, cols]

    for d in NEAR + GROUPS[9:]:
        wait_bytes(blk, z_ss.at[d])
    wait_bytes(G.at[0:3, :, 0, :, 0], f_ss)
    wait_bytes(G.at[0:3, :, 0], s_ss)
    wait_bytes(G.at[:, :, 0], c_ss)
    for done in given:
        done()


def on_device(amplitudes, driving, ladder, block_mask, virt_energy, occ_energy):
    vmem = pl.BlockSpec(memory_space=pltpu.VMEM)
    smem = pl.BlockSpec(memory_space=pltpu.SMEM)
    hbm = pl.BlockSpec(memory_space=pltpu.HBM)
    dma = pltpu.SemaphoreType.DMA
    return pl.pallas_call(
        kernel,
        out_shape=pltpu.VMEM(amplitudes.shape, F32),
        in_specs=[hbm, hbm, vmem, smem, smem, smem],
        out_specs=vmem,
        scratch_shapes=[
            pltpu.VMEM((NH, NH, 2, NX, NX, 16, 128), BF16),
            pltpu.VMEM((16, 4, 16, IJ), BF16),
            pltpu.VMEM((IJ, IJ), BF16),
            pltpu.VMEM((512, 512), BF16),
            pltpu.VMEM((16, 128), BF16),
            pltpu.VMEM(amplitudes.shape, F32),
            pltpu.VMEM(driving.shape, BF16),
            pltpu.VMEM(amplitudes.shape, BF16),
            pltpu.VMEM((ROWS, IJ), F32),
            pltpu.VMEM((ROWS, IJ), BF16),
            pltpu.VMEM((ROWS, IJ), BF16),
            pltpu.VMEM((2 * ROWS, IJ), BF16),
            pltpu.VMEM((ROWS, IJ), BF16),
            pltpu.VMEM((ROWS, IJ), F32),
            pltpu.VMEM((ROWS, IJ), BF16),
            pltpu.VMEM((CHUNKS, 2, 8, 8, COLS), BF16),
            pltpu.VMEM((CHUNKS, 2, 8, 8, COLS), BF16),
            pltpu.VMEM((IJ // 128, ROWS, 128), F32),
            pltpu.VMEM((2, EARLY, 8, IJ), BF16),
            pltpu.VMEM((2, EARLY, 8, IJ), BF16),
            pltpu.VMEM((EROWS, IJ), F32),
            pltpu.VMEM((EROWS, IJ), BF16),
            pltpu.VMEM((EROWS, IJ), BF16),
            pltpu.VMEM((2 * EROWS, IJ), BF16),
            pltpu.VMEM((EROWS, IJ), BF16),
            pltpu.VMEM((EROWS, IJ), BF16),
            dma((2,)),
            dma((2, 2)),
            dma((2, 2)),
            dma((NZ,)),
            dma((NZ,)),
            dma(()),
            dma((NZ,)),
            dma(()),
            dma((NZ,)),
            dma(()),
            dma((NZ,)),
            dma((CHUNKS, 2)),
            dma((CHUNKS, 2)),
        ],
        compiler_params=pltpu.CompilerParams(collective_id=0, has_side_effects=True),
    )(amplitudes, driving, ladder.T, block_mask, virt_energy, occ_energy)


def solution(mesh):
    placed = (P("aa", "ba", None), P("aa", "ba", None), P("aa", "ba"), P(), P(), P())
    return jax.shard_map(
        on_device, mesh=mesh, in_specs=placed, out_specs=P("aa", "ba", None), check_vma=False
    )
```

```python
import jax
import jax.numpy as jnp
from jax import lax
from jax.experimental import pallas as pl
from jax.experimental.pallas import tpu as pltpu
from jax.sharding import PartitionSpec as P

MESH = pl.DeviceIdType.MESH
F32 = jnp.float32
BF16 = jnp.bfloat16
O = 32
NX = 4
NH = 4
NZ = 16
IJ = 1024
ROWS = 128
COLS = 256
CHUNKS = IJ // COLS
NEAR = (1, 15, 2, 14, 3, 13, 4, 12)
GROUPS = (0,) + NEAR + (5, 11, 6, 10, 7, 9, 8)
EARLY = 3
EROWS = 2 * EARLY * 8
LAG = 4
RAW_AT = 0


def plan():
    events = [(0, n) for n in range(NZ)] + [(1, n) for n in range(NZ)]
    for n in range(NZ + LAG):
        if n == RAW_AT:
            events.append((4, 0))
        if n < NZ:
            events.append((2, n))
        if n >= LAG:
            events.append((3, n - LAG))
    return events


def iota(shape, dim):
    return lax.broadcasted_iota(jnp.int32, shape, dim)


def onehot(cond):
    return jnp.where(cond, 1.0, 0.0).astype(BF16)


def dot(a, b):
    return jnp.dot(a, b, preferred_element_type=F32)


def kernel(
    amp_hbm, drv_hbm, lad_hbm, mask_hbm, ve_hbm, oe_hbm, out,
    lad, mask, ve, oe,
    G, W, perm, shuf, blk, amp, drv, abt, rden, ab, tb, lhs, cb, x1, x2b, zsend, zrecv, vs,
    araw, draw, rden2, ab2, tb2, lhs2, cb2, x2b2, in_s, r_ss, r_rs, z_ss, z_rs, f_ss, f_rs, s_ss, s_rs, c_ss, c_rs, e_ss, e_rs,
):
    p = lax.axis_index("aa")
    q = lax.axis_index("ba")
    zh, x = lax.div(p, NX), lax.rem(p, NX)
    zl = lax.div(q, 2 * NX)
    y = lax.rem(lax.div(q, 2), NX)
    k = lax.rem(q, 2)
    z = zh * NH + zl

    def dev(z_, x_, y_, k_):
        return (lax.div(z_, NH) * NX + x_, lax.rem(z_, NH) * (2 * NX) + y_ * 2 + k_)

    def rot(v, d, n):
        return lax.rem(v + d, n)

    x_peers = [dev(z, rot(x, d, NX), y, k) for d in (2, 1, 3)]
    y_peers = [dev(z, x, rot(y, d, NX), k) for d in (2, 1, 3)]
    sibling = dev(z, x, y, 1 - k)
    z_peer = {d: dev(rot(z, d, NZ), x, y, k) for d in NEAR}

    barrier = pltpu.get_barrier_semaphore()
    peers = [z_peer[d] for d in reversed(NEAR)] + x_peers + y_peers + [sibling]
    peers += [dev(z, rot(x, d, NX), y, 1 - k) for d in (2, 1, 3)]
    peers += [dev(z, x, rot(y, d, NX), 1 - k) for d in (2, 1, 3)]
    for peer in peers:
        pl.semaphore_signal(barrier, inc=1, device_id=peer, device_id_type=MESH)

    pairs = ((lad_hbm, lad), (mask_hbm, mask), (ve_hbm, ve), (oe_hbm, oe), (amp_hbm, amp), (drv_hbm, drv))
    loads = [pltpu.make_async_copy(src, dst, in_s.at[i]) for i, (src, dst) in enumerate(pairs)]
    for load in loads:
        load.start()

    eye = onehot(iota((64, 64), 0) == iota((64, 64), 1))
    spread = onehot((iota((O, 128), 1) & (O - 1)) == iota((O, 128), 0))
    group = iota((16, 128), 1) >> 5
    for load in loads[:4]:
        load.wait()
    keep = mask[p, lax.div(q, 2)].astype(F32)
    rows = lax.dot_general(
        eye, lad[...], (((1,), (1,)), ((), ())), preferred_element_type=F32
    ).astype(BF16)
    four = dot(rows, spread)
    packed = four[0:16]
    for t in range(1, 4):
        packed = jnp.where(group == t, four[16 * t : 16 * t + 16], packed)
    packed = (packed * keep).astype(BF16)
    blk[...] = packed
    G[zh, zl, k, x, y] = packed

    def copy(src, dst, ss, rs, to):
        return pltpu.make_async_remote_copy(
            src_ref=src, dst_ref=dst, send_sem=ss, recv_sem=rs, device_id=to, device_id_type=MESH
        )

    def wait_bytes(ref, sem):
        pltpu.make_async_copy(ref, ref, sem).wait()

    pl.semaphore_wait(barrier, len(peers))
    for d in reversed(NEAR):
        copy(blk, G.at[zh, zl, k, x, y], z_ss.at[d], z_rs.at[d], z_peer[d]).start()

    def plane(e):
        src_z = rot(z, NZ - e, NZ)
        return lax.div(src_z, NH), lax.rem(src_z, NH)

    def first(n):
        e = GROUPS[n]
        h_, l_ = plane(e)
        piece = G.at[h_, l_, k, x, y]
        if e:
            wait_bytes(blk, z_rs.at[e])
        if 1 <= e <= 4:
            copy(piece, piece, z_ss.at[e + 4], z_rs.at[e + 4], z_peer[4]).start()
        if 13 <= e <= 15:
            copy(piece, piece, z_ss.at[e - 4], z_rs.at[e - 4], z_peer[12]).start()
        for to in x_peers if n % 2 == 0 else y_peers:
            copy(piece, piece, f_ss, f_rs.at[n], to).start()

    def second(n):
        h_, l_ = plane(GROUPS[n])
        wait_bytes(G.at[0, 0, 0, 0, 0:3], f_rs.at[n])
        if n % 2 == 0:
            piece, to_all = G.at[h_, l_, k, :, y], y_peers
        else:
            piece, to_all = G.at[h_, l_, k, x], x_peers
        for to in to_all:
            copy(piece, piece, s_ss, s_rs.at[n], to).start()

    def third(n):
        h_, l_ = plane(GROUPS[n])
        wait_bytes(G.at[0, 0, 0, 0:3], s_rs.at[n])
        piece = G.at[h_, l_, k]
        copy(piece, piece, c_ss, c_rs.at[n], sibling).start()

    def use(n):
        h_, l_ = plane(GROUPS[n])
        wait_bytes(G.at[0, 0, 0], c_rs.at[n])
        wide = jnp.concatenate(
            [
                jnp.concatenate(
                    [G[h_, l_, j % 2, :, 2 * g + j // 2].reshape(64, 128) for j in range(4)], axis=1
                )
                for g in range(2)
            ],
            axis=0,
        )
        moved = dot(wide, shuf[...]).astype(BF16)
        cols = pl.ds(pl.multiple_of(l_ * COLS, COLS), COLS)
        for t in range(4):
            W[pl.ds(h_ * NX, NX), t, :, cols] = jnp.concatenate(
                [moved[64 * g : 64 * g + 64, 128 * t : 128 * t + 128] for g in range(2)], axis=1
            ).reshape(NX, 16, COLS)

    def prepare():
        r = iota((512, 512), 0)
        c = iota((512, 512), 1)
        shuf[...] = onehot(c == ((r >> 5) & 3) * 128 + (r >> 7) * 32 + (r & 31))
        loads[4].wait()
        ab[...] = amp[...].reshape(ROWS, IJ).astype(BF16)
        abt[...] = amp[...].astype(BF16)

        @pl.loop(0, 8)
        def _(i):
            r = iota((128, IJ), 0) + i * 128
            c = iota((128, IJ), 1)
            perm[pl.ds(pl.multiple_of(i * 128, 128), 128), :] = onehot(
                r == (c & (O - 1)) * O + (c >> 5)
            )

        lane = iota((8, IJ), 1)
        pair = jnp.zeros((8, IJ), F32)
        for i in range(O):
            e = oe[i]
            pair = pair + jnp.where((lane >> 5) == i, e, 0.0) + jnp.where((lane & (O - 1)) == i, e, 0.0)
        row = iota((8, IJ), 0)

        def over(first_b):
            base = -pair
            for b in range(8):
                base = base + jnp.where(row == b, ve[first_b + b], 0.0)
            return base

        base = over(q * 8)
        for a in range(16):
            rden[8 * a : 8 * a + 8, :] = 1.0 / (base + ve[p * 16 + a])
        for s in range(2):
            base = over(p * 16 + 8 * s)
            for a in range(EARLY):
                r = 8 * (s * EARLY + a)
                rden2[r : r + 8, :] = 1.0 / (base + ve[q * 8 + a])
        loads[5].wait()

    def give(src, dst, ss, rs, h):
        to = (lax.div(q, 2), 2 * p + h)
        own = jnp.logical_and(to[0] == p, to[1] == q)
        send = copy(src, dst, ss, rs, to)

        @pl.when(jnp.logical_not(own))
        def _():
            send.start()

        @pl.when(own)
        def _():
            pltpu.make_async_copy(src, dst, rs).start()

        def done():
            @pl.when(jnp.logical_not(own))
            def _():
                send.wait_send()

        return done

    given = []

    def early(_):
        for h in range(2):
            for j, (src, dst) in enumerate(((abt, araw), (drv, draw))):
                piece = src.at[8 * h : 8 * h + EARLY]
                given.append(give(piece, dst.at[k], r_ss.at[h, j], r_rs.at[k, j], h))

    steps = [first, second, third, use, early]
    for i, (kind, n) in enumerate(plan()):
        if i == 9:
            prepare()
        steps[kind](n)

    def columns(n):
        if isinstance(n, int):
            return slice(n * COLS, (n + 1) * COLS)
        return pl.ds(pl.multiple_of(n * COLS, COLS), COLS)

    def w_cols(n):
        return W[:, :, :, columns(n)].reshape(IJ, COLS)

    def halves(count, tile, drive, over_den, t_, b_, c_, two):
        @pl.loop(0, CHUNKS)
        def _(n):
            t1 = dot(tile[...], w_cols(n))
            t_[:, columns(n)] = t1.astype(BF16)
            b1 = (drive(n) + t1) * over_den[:, columns(n)]
            high = b1.astype(BF16)
            b_[0:count, columns(n)] = high
            b_[count : 2 * count, columns(n)] = (b1 - high.astype(F32)).astype(BF16)

        @pl.loop(0, CHUNKS)
        def _(n):
            turned = dot(t_[...], perm[:, columns(n)]) * over_den[:, columns(n)]
            c_[:, columns(n)] = turned.astype(BF16)

        @pl.loop(0, CHUNKS)
        def _(n):
            two[:, columns(n)] = dot(c_[...], w_cols(n)).astype(BF16)

    def joined(n, count, b_, two):
        both = dot(b_[...], w_cols(n))
        return both[0:count] + both[count : 2 * count] + dot(two[...], perm[:, columns(n)])

    def drive(n):
        return drv[:, :, columns(n)].astype(F32).reshape(ROWS, COLS)

    halves(ROWS, ab, drive, rden, tb, lhs, cb, x2b)

    for n in range(CHUNKS):
        cols = slice(n * COLS, (n + 1) * COLS)
        zz = joined(n, ROWS, lhs, x2b)
        x1[:, cols] = drv[:, :, cols].astype(F32).reshape(ROWS, COLS) + zz
        zsend[n] = zz.reshape(2, 8, 8, COLS).astype(BF16)
        for h in range(2):
            given.append(
                give(
                    zsend.at[n, h, EARLY:8], zrecv.at[n, k, EARLY:8], e_ss.at[n, h], e_rs.at[n, k], h
                )
            )

    for s in range(2):
        for j, dst in enumerate((araw, draw)):
            wait_bytes(dst.at[s], r_rs.at[s, j])
    ab2[...] = araw[...].astype(F32).reshape(EROWS, IJ).astype(BF16)

    def early_drive(n):
        return draw[:, :, :, columns(n)].astype(F32).reshape(EROWS, COLS)

    halves(EROWS, ab2, early_drive, rden2, tb2, lhs2, cb2, x2b2)
    for n in range(CHUNKS):
        zz = joined(n, EROWS, lhs2, x2b2)
        zrecv[n, :, 0:EARLY] = zz.reshape(2, EARLY, 8, COLS).astype(BF16)

    for n in range(CHUNKS):
        for s in range(2):
            wait_bytes(zrecv.at[n, s, EARLY:8], e_rs.at[n, s])
        got = zrecv[n].astype(F32).reshape(ROWS, COLS).astype(BF16)
        for m in range(CHUNKS):
            turned = dot(got, perm[n * COLS : (n + 1) * COLS, m * COLS : (m + 1) * COLS])
            for c in range(COLS // 128):
                part = turned[:, 128 * c : 128 * c + 128]
                if n:
                    vs[m * (COLS // 128) + c] += part
                else:
                    vs[m * (COLS // 128) + c] = part

    @pl.loop(0, IJ // 128)
    def _(c):
        cols = pl.ds(pl.multiple_of(c * 128, 128), 128)
        for s in range(2):
            for b in range(8):
                r = 8 * (8 * s + b)
                other = vs[c, pl.ds(64 * s + b, 8, stride=8), :]
                out[8 * s + b, :, cols] = (x1[r : r + 8, cols] + other) * rden[r : r + 8, cols]

    for d in NEAR + GROUPS[9:]:
        wait_bytes(blk, z_ss.at[d])
    wait_bytes(G.at[0:3, :, 0, :, 0], f_ss)
    wait_bytes(G.at[0:3, :, 0], s_ss)
    wait_bytes(G.at[:, :, 0], c_ss)
    for done in given:
        done()


def on_device(amplitudes, driving, ladder, block_mask, virt_energy, occ_energy):
    vmem = pl.BlockSpec(memory_space=pltpu.VMEM)
    hbm = pl.BlockSpec(memory_space=pltpu.HBM)
    dma = pltpu.SemaphoreType.DMA
    return pl.pallas_call(
        kernel,
        out_shape=pltpu.VMEM(amplitudes.shape, F32),
        in_specs=[hbm] * 6,
        out_specs=vmem,
        scratch_shapes=[
            pltpu.VMEM((O, 64), BF16),
            pltpu.SMEM(block_mask.shape, jnp.int32),
            pltpu.SMEM(virt_energy.shape, F32),
            pltpu.SMEM(occ_energy.shape, F32),
            pltpu.VMEM((NH, NH, 2, NX, NX, 16, 128), BF16),
            pltpu.VMEM((16, 4, 16, IJ), BF16),
            pltpu.VMEM((IJ, IJ), BF16),
            pltpu.VMEM((512, 512), BF16),
            pltpu.VMEM((16, 128), BF16),
            pltpu.VMEM(amplitudes.shape, F32),
            pltpu.VMEM(driving.shape, BF16),
            pltpu.VMEM(amplitudes.shape, BF16),
            pltpu.VMEM((ROWS, IJ), F32),
            pltpu.VMEM((ROWS, IJ), BF16),
            pltpu.VMEM((ROWS, IJ), BF16),
            pltpu.VMEM((2 * ROWS, IJ), BF16),
            pltpu.VMEM((ROWS, IJ), BF16),
            pltpu.VMEM((ROWS, IJ), F32),
            pltpu.VMEM((ROWS, IJ), BF16),
            pltpu.VMEM((CHUNKS, 2, 8, 8, COLS), BF16),
            pltpu.VMEM((CHUNKS, 2, 8, 8, COLS), BF16),
            pltpu.VMEM((IJ // 128, ROWS, 128), F32),
            pltpu.VMEM((2, EARLY, 8, IJ), BF16),
            pltpu.VMEM((2, EARLY, 8, IJ), BF16),
            pltpu.VMEM((EROWS, IJ), F32),
            pltpu.VMEM((EROWS, IJ), BF16),
            pltpu.VMEM((EROWS, IJ), BF16),
            pltpu.VMEM((2 * EROWS, IJ), BF16),
            pltpu.VMEM((EROWS, IJ), BF16),
            pltpu.VMEM((EROWS, IJ), BF16),
            dma((6,)),
            dma((2, 2)),
            dma((2, 2)),
            dma((NZ,)),
            dma((NZ,)),
            dma(()),
            dma((NZ,)),
            dma(()),
            dma((NZ,)),
            dma(()),
            dma((NZ,)),
            dma((CHUNKS, 2)),
            dma((CHUNKS, 2)),
        ],
        compiler_params=pltpu.CompilerParams(collective_id=0, has_side_effects=True),
    )(amplitudes, driving, ladder.T, block_mask, virt_energy, occ_energy)


def solution(mesh):
    placed = (P("aa", "ba", None), P("aa", "ba", None), P("aa", "ba"), P(), P(), P())
    return jax.shard_map(
        on_device, mesh=mesh, in_specs=placed, out_specs=P("aa", "ba", None), check_vma=False
    )
```

```python
import jax
import jax.numpy as jnp
from jax import lax
from jax.experimental import pallas as pl
from jax.experimental.pallas import tpu as pltpu
from jax.sharding import PartitionSpec as P

MESH = pl.DeviceIdType.MESH
F32 = jnp.float32
BF16 = jnp.bfloat16
O = 32
NX = 4
NH = 4
NZ = 16
IJ = 1024
ROWS = 128
COLS = 256
CHUNKS = IJ // COLS
NEAR = (1, 15, 2, 14, 3, 13, 4, 12)
GROUPS = (0,) + NEAR + (5, 11, 6, 10, 7, 9, 8)
EARLY = 3
EROWS = 2 * EARLY * 8
LAG = 4
RAW_AT = 0


def plan():
    events = [(0, n) for n in range(NZ)] + [(1, n) for n in range(NZ)]
    for n in range(NZ + LAG):
        if n == RAW_AT:
            events.append((4, 0))
        if n < NZ:
            events.append((2, n))
        if n >= LAG:
            events.append((3, n - LAG))
    return events


def iota(shape, dim):
    return lax.broadcasted_iota(jnp.int32, shape, dim)


def onehot(cond):
    return jnp.where(cond, 1.0, 0.0).astype(BF16)


def dot(a, b):
    return jnp.dot(a, b, preferred_element_type=F32)


def kernel(
    amp_hbm, drv_hbm, lad_hbm, mask_hbm, ve_hbm, oe_hbm, out,
    lad, mask, ve, oe,
    G, W, perm, shuf, blk, amp, drv, abt, rden, ab, tb, lhs, cb, x1, x2b, zsend, zrecv, vs,
    araw, draw, rden2, ab2, tb2, lhs2, cb2, x2b2, in_s, r_ss, r_rs, z_ss, z_rs, f_ss, f_rs, s_ss, s_rs, c_ss, c_rs, e_ss, e_rs,
):
    p = lax.axis_index("aa")
    q = lax.axis_index("ba")
    zh, x = lax.div(p, NX), lax.rem(p, NX)
    zl = lax.div(q, 2 * NX)
    y = lax.rem(lax.div(q, 2), NX)
    k = lax.rem(q, 2)
    z = zh * NH + zl

    def dev(z_, x_, y_, k_):
        return (lax.div(z_, NH) * NX + x_, lax.rem(z_, NH) * (2 * NX) + y_ * 2 + k_)

    def rot(v, d, n):
        return lax.rem(v + d, n)

    x_peers = [dev(z, rot(x, d, NX), y, k) for d in (2, 1, 3)]
    y_peers = [dev(z, x, rot(y, d, NX), k) for d in (2, 1, 3)]
    sibling = dev(z, x, y, 1 - k)
    z_peer = {d: dev(rot(z, d, NZ), x, y, k) for d in NEAR}

    barrier = pltpu.get_barrier_semaphore()
    peers = [z_peer[d] for d in reversed(NEAR)] + x_peers + y_peers + [sibling]
    peers += [dev(z, rot(x, d, NX), y, 1 - k) for d in (2, 1, 3)]
    peers += [dev(z, x, rot(y, d, NX), 1 - k) for d in (2, 1, 3)]
    for peer in peers:
        pl.semaphore_signal(barrier, inc=1, device_id=peer, device_id_type=MESH)

    pairs = ((lad_hbm, lad), (mask_hbm, mask), (ve_hbm, ve), (oe_hbm, oe), (amp_hbm, amp), (drv_hbm, drv))
    loads = [pltpu.make_async_copy(src, dst, in_s.at[i]) for i, (src, dst) in enumerate(pairs)]
    for load in loads:
        load.start()

    eye = onehot(iota((64, 64), 0) == iota((64, 64), 1))
    spread = onehot((iota((O, 128), 1) & (O - 1)) == iota((O, 128), 0))
    group = iota((16, 128), 1) >> 5
    for load in loads[:4]:
        load.wait()
    keep = mask[p, lax.div(q, 2)].astype(F32)
    rows = lax.dot_general(
        eye, lad[...], (((1,), (1,)), ((), ())), preferred_element_type=F32
    ).astype(BF16)
    four = dot(rows, spread)
    packed = four[0:16]
    for t in range(1, 4):
        packed = jnp.where(group == t, four[16 * t : 16 * t + 16], packed)
    packed = (packed * keep).astype(BF16)
    blk[...] = packed
    G[zh, zl, k, x, y] = packed

    def copy(src, dst, ss, rs, to):
        return pltpu.make_async_remote_copy(
            src_ref=src, dst_ref=dst, send_sem=ss, recv_sem=rs, device_id=to, device_id_type=MESH
        )

    def wait_bytes(ref, sem):
        pltpu.make_async_copy(ref, ref, sem).wait()

    pl.semaphore_wait(barrier, len(peers))
    for d in reversed(NEAR):
        copy(blk, G.at[zh, zl, k, x, y], z_ss.at[d], z_rs.at[d], z_peer[d]).start()

    def plane(e):
        src_z = rot(z, NZ - e, NZ)
        return lax.div(src_z, NH), lax.rem(src_z, NH)

    def first(n):
        e = GROUPS[n]
        h_, l_ = plane(e)
        piece = G.at[h_, l_, k, x, y]
        if e:
            wait_bytes(blk, z_rs.at[e])
        if 1 <= e <= 4:
            copy(piece, piece, z_ss.at[e + 4], z_rs.at[e + 4], z_peer[4]).start()
        if 13 <= e <= 15:
            copy(piece, piece, z_ss.at[e - 4], z_rs.at[e - 4], z_peer[12]).start()
        for to in x_peers if n % 2 == 0 else y_peers:
            copy(piece, piece, f_ss, f_rs.at[n], to).start()

    def second(n):
        h_, l_ = plane(GROUPS[n])
        wait_bytes(G.at[0, 0, 0, 0, 0:3], f_rs.at[n])
        if n % 2 == 0:
            piece, to_all = G.at[h_, l_, k, :, y], y_peers
        else:
            piece, to_all = G.at[h_, l_, k, x], x_peers
        for to in to_all:
            copy(piece, piece, s_ss, s_rs.at[n], to).start()

    def third(n):
        h_, l_ = plane(GROUPS[n])
        wait_bytes(G.at[0, 0, 0, 0:3], s_rs.at[n])
        piece = G.at[h_, l_, k]
        copy(piece, piece, c_ss, c_rs.at[n], sibling).start()

    def use(n):
        h_, l_ = plane(GROUPS[n])
        wait_bytes(G.at[0, 0, 0], c_rs.at[n])
        wide = jnp.concatenate(
            [
                jnp.concatenate(
                    [G[h_, l_, j % 2, :, 2 * g + j // 2].reshape(64, 128) for j in range(4)], axis=1
                )
                for g in range(2)
            ],
            axis=0,
        )
        moved = dot(wide, shuf[...]).astype(BF16)
        cols = pl.ds(pl.multiple_of(l_ * COLS, COLS), COLS)
        for t in range(4):
            W[pl.ds(h_ * NX, NX), t, :, cols] = jnp.concatenate(
                [moved[64 * g : 64 * g + 64, 128 * t : 128 * t + 128] for g in range(2)], axis=1
            ).reshape(NX, 16, COLS)

    def prepare():
        r = iota((512, 512), 0)
        c = iota((512, 512), 1)
        shuf[...] = onehot(c == ((r >> 5) & 3) * 128 + (r >> 7) * 32 + (r & 31))
        loads[4].wait()
        ab[...] = amp[...].reshape(ROWS, IJ).astype(BF16)
        abt[...] = amp[...].astype(BF16)

        @pl.loop(0, 8)
        def _(i):
            r = iota((128, IJ), 0) + i * 128
            c = iota((128, IJ), 1)
            perm[pl.ds(pl.multiple_of(i * 128, 128), 128), :] = onehot(
                r == (c & (O - 1)) * O + (c >> 5)
            )

        lane = iota((8, IJ), 1)
        pair = jnp.zeros((8, IJ), F32)
        for i in range(O):
            e = oe[i]
            pair = pair + jnp.where((lane >> 5) == i, e, 0.0) + jnp.where((lane & (O - 1)) == i, e, 0.0)
        row = iota((8, IJ), 0)

        def over(first_b):
            base = -pair
            for b in range(8):
                base = base + jnp.where(row == b, ve[first_b + b], 0.0)
            return base

        base = over(q * 8)
        for a in range(16):
            rden[8 * a : 8 * a + 8, :] = 1.0 / (base + ve[p * 16 + a])
        for s in range(2):
            base = over(p * 16 + 8 * s)
            for a in range(EARLY):
                r = 8 * (s * EARLY + a)
                rden2[r : r + 8, :] = 1.0 / (base + ve[q * 8 + a])
        loads[5].wait()

    def give(src, dst, ss, rs, h):
        to = (lax.div(q, 2), 2 * p + h)
        own = jnp.logical_and(to[0] == p, to[1] == q)
        send = copy(src, dst, ss, rs, to)

        @pl.when(jnp.logical_not(own))
        def _():
            send.start()

        @pl.when(own)
        def _():
            pltpu.make_async_copy(src, dst, rs).start()

        def done():
            @pl.when(jnp.logical_not(own))
            def _():
                send.wait_send()

        return done

    given = []

    def early(_):
        for h in range(2):
            for j, (src, dst) in enumerate(((abt, araw), (drv, draw))):
                piece = src.at[8 * h : 8 * h + EARLY]
                given.append(give(piece, dst.at[k], r_ss.at[h, j], r_rs.at[k, j], h))

    steps = [first, second, third, use, early]
    for i, (kind, n) in enumerate(plan()):
        if i == 9:
            prepare()
        steps[kind](n)

    def columns(n):
        if isinstance(n, int):
            return slice(n * COLS, (n + 1) * COLS)
        return pl.ds(pl.multiple_of(n * COLS, COLS), COLS)

    def w_cols(n):
        return W[:, :, :, columns(n)].reshape(IJ, COLS)

    def halves(count, tile, drive, over_den, t_, b_, c_, two):
        for n in range(CHUNKS):
            t1 = dot(tile[...], w_cols(n))
            t_[:, columns(n)] = t1.astype(BF16)
            b1 = (drive(n) + t1) * over_den[:, columns(n)]
            high = b1.astype(BF16)
            b_[0:count, columns(n)] = high
            b_[count : 2 * count, columns(n)] = (b1 - high.astype(F32)).astype(BF16)

        for n in range(CHUNKS):
            turned = dot(t_[...], perm[:, columns(n)]) * over_den[:, columns(n)]
            c_[:, columns(n)] = turned.astype(BF16)

        for n in range(CHUNKS):
            two[:, columns(n)] = dot(c_[...], w_cols(n)).astype(BF16)

    def joined(n, count, b_, two):
        both = dot(b_[...], w_cols(n))
        return both[0:count] + both[count : 2 * count] + dot(two[...], perm[:, columns(n)])

    def drive(n):
        return drv[:, :, columns(n)].astype(F32).reshape(ROWS, COLS)

    halves(ROWS, ab, drive, rden, tb, lhs, cb, x2b)

    for n in range(CHUNKS):
        cols = slice(n * COLS, (n + 1) * COLS)
        zz = joined(n, ROWS, lhs, x2b)
        zsend[n] = zz.reshape(2, 8, 8, COLS).astype(BF16)
        for h in range(2):
            given.append(
                give(
                    zsend.at[n, h, EARLY:8], zrecv.at[n, k, EARLY:8], e_ss.at[n, h], e_rs.at[n, k], h
                )
            )
        x1[:, cols] = drv[:, :, cols].astype(F32).reshape(ROWS, COLS) + zz

    for s in range(2):
        for j, dst in enumerate((araw, draw)):
            wait_bytes(dst.at[s], r_rs.at[s, j])
    ab2[...] = araw[...].astype(F32).reshape(EROWS, IJ).astype(BF16)

    def early_drive(n):
        return draw[:, :, :, columns(n)].astype(F32).reshape(EROWS, COLS)

    halves(EROWS, ab2, early_drive, rden2, tb2, lhs2, cb2, x2b2)
    for n in range(CHUNKS):
        zz = joined(n, EROWS, lhs2, x2b2)
        zrecv[n, :, 0:EARLY] = zz.reshape(2, EARLY, 8, COLS).astype(BF16)

    for n in range(CHUNKS):
        for s in range(2):
            wait_bytes(zrecv.at[n, s, EARLY:8], e_rs.at[n, s])
        got = zrecv[n].astype(F32).reshape(ROWS, COLS).astype(BF16)
        for m in range(CHUNKS):
            turned = dot(got, perm[n * COLS : (n + 1) * COLS, m * COLS : (m + 1) * COLS])
            for c in range(COLS // 128):
                part = turned[:, 128 * c : 128 * c + 128]
                if n:
                    vs[m * (COLS // 128) + c] += part
                else:
                    vs[m * (COLS // 128) + c] = part

    @pl.loop(0, IJ // 128)
    def _(c):
        cols = pl.ds(pl.multiple_of(c * 128, 128), 128)
        for s in range(2):
            for b in range(8):
                r = 8 * (8 * s + b)
                other = vs[c, pl.ds(64 * s + b, 8, stride=8), :]
                out[8 * s + b, :, cols] = (x1[r : r + 8, cols] + other) * rden[r : r + 8, cols]

    for d in NEAR + GROUPS[9:]:
        wait_bytes(blk, z_ss.at[d])
    wait_bytes(G.at[0:3, :, 0, :, 0], f_ss)
    wait_bytes(G.at[0:3, :, 0], s_ss)
    wait_bytes(G.at[:, :, 0], c_ss)
    for done in given:
        done()


def on_device(amplitudes, driving, ladder, block_mask, virt_energy, occ_energy):
    vmem = pl.BlockSpec(memory_space=pltpu.VMEM)
    hbm = pl.BlockSpec(memory_space=pltpu.HBM)
    dma = pltpu.SemaphoreType.DMA
    return pl.pallas_call(
        kernel,
        out_shape=pltpu.VMEM(amplitudes.shape, F32),
        in_specs=[hbm] * 6,
        out_specs=vmem,
        scratch_shapes=[
            pltpu.VMEM((O, 64), BF16),
            pltpu.SMEM(block_mask.shape, jnp.int32),
            pltpu.SMEM(virt_energy.shape, F32),
            pltpu.SMEM(occ_energy.shape, F32),
            pltpu.VMEM((NH, NH, 2, NX, NX, 16, 128), BF16),
            pltpu.VMEM((16, 4, 16, IJ), BF16),
            pltpu.VMEM((IJ, IJ), BF16),
            pltpu.VMEM((512, 512), BF16),
            pltpu.VMEM((16, 128), BF16),
            pltpu.VMEM(amplitudes.shape, F32),
            pltpu.VMEM(driving.shape, BF16),
            pltpu.VMEM(amplitudes.shape, BF16),
            pltpu.VMEM((ROWS, IJ), F32),
            pltpu.VMEM((ROWS, IJ), BF16),
            pltpu.VMEM((ROWS, IJ), BF16),
            pltpu.VMEM((2 * ROWS, IJ), BF16),
            pltpu.VMEM((ROWS, IJ), BF16),
            pltpu.VMEM((ROWS, IJ), F32),
            pltpu.VMEM((ROWS, IJ), BF16),
            pltpu.VMEM((CHUNKS, 2, 8, 8, COLS), BF16),
            pltpu.VMEM((CHUNKS, 2, 8, 8, COLS), BF16),
            pltpu.VMEM((IJ // 128, ROWS, 128), F32),
            pltpu.VMEM((2, EARLY, 8, IJ), BF16),
            pltpu.VMEM((2, EARLY, 8, IJ), BF16),
            pltpu.VMEM((EROWS, IJ), F32),
            pltpu.VMEM((EROWS, IJ), BF16),
            pltpu.VMEM((EROWS, IJ), BF16),
            pltpu.VMEM((2 * EROWS, IJ), BF16),
            pltpu.VMEM((EROWS, IJ), BF16),
            pltpu.VMEM((EROWS, IJ), BF16),
            dma((6,)),
            dma((2, 2)),
            dma((2, 2)),
            dma((NZ,)),
            dma((NZ,)),
            dma(()),
            dma((NZ,)),
            dma(()),
            dma((NZ,)),
            dma(()),
            dma((NZ,)),
            dma((CHUNKS, 2)),
            dma((CHUNKS, 2)),
        ],
        compiler_params=pltpu.CompilerParams(collective_id=0, has_side_effects=True),
    )(amplitudes, driving, ladder.T, block_mask, virt_energy, occ_energy)


def solution(mesh):
    placed = (P("aa", "ba", None), P("aa", "ba", None), P("aa", "ba"), P(), P(), P())
    return jax.shard_map(
        on_device, mesh=mesh, in_specs=placed, out_specs=P("aa", "ba", None), check_vma=False
    )
```

```python
import jax
import jax.numpy as jnp
from jax import lax
from jax.experimental import pallas as pl
from jax.experimental.pallas import tpu as pltpu
from jax.sharding import PartitionSpec as P

MESH = pl.DeviceIdType.MESH
F32 = jnp.float32
BF16 = jnp.bfloat16
O = 32
NX = 4
NH = 4
NZ = 16
IJ = 1024
ROWS = 128
COLS = 256
CHUNKS = IJ // COLS
NEAR = (1, 15, 2, 14, 3, 13, 4, 12)
GROUPS = (0,) + NEAR + (5, 11, 6, 10, 7, 9, 8)
EARLY = 3
EROWS = 2 * EARLY * 8
LAG = 4
RAW_AT = 0


def plan():
    events = [(0, n) for n in range(NZ)] + [(1, n) for n in range(NZ)]
    for n in range(NZ + LAG):
        if n == RAW_AT:
            events.append((4, 0))
        if n < NZ:
            events.append((2, n))
        if n >= LAG:
            events.append((3, n - LAG))
    return events


def iota(shape, dim):
    return lax.broadcasted_iota(jnp.int32, shape, dim)


def onehot(cond):
    return jnp.where(cond, 1.0, 0.0).astype(BF16)


def dot(a, b):
    return jnp.dot(a, b, preferred_element_type=F32)


def kernel(
    amp_hbm, drv_hbm, lad_hbm, mask_hbm, ve_hbm, oe_hbm, out,
    lad, mask, ve, oe,
    G, W, perm, shuf, blk, amp, drv, abt, rden, ab, tb, lhs, cb, x1, x2b, zsend, zrecv, vs,
    araw, draw, rden2, ab2, tb2, lhs2, cb2, x2b2, in_s, r_ss, r_rs, z_ss, z_rs, f_ss, f_rs, s_ss, s_rs, c_ss, c_rs, e_ss, e_rs,
):
    p = lax.axis_index("aa")
    q = lax.axis_index("ba")
    zh, x = lax.div(p, NX), lax.rem(p, NX)
    zl = lax.div(q, 2 * NX)
    y = lax.rem(lax.div(q, 2), NX)
    k = lax.rem(q, 2)
    z = zh * NH + zl

    def dev(z_, x_, y_, k_):
        return (lax.div(z_, NH) * NX + x_, lax.rem(z_, NH) * (2 * NX) + y_ * 2 + k_)

    def rot(v, d, n):
        return lax.rem(v + d, n)

    x_peers = [dev(z, rot(x, d, NX), y, k) for d in (2, 1, 3)]
    y_peers = [dev(z, x, rot(y, d, NX), k) for d in (2, 1, 3)]
    sibling = dev(z, x, y, 1 - k)
    z_peer = {d: dev(rot(z, d, NZ), x, y, k) for d in NEAR}

    barrier = pltpu.get_barrier_semaphore()
    peers = [z_peer[d] for d in reversed(NEAR)] + x_peers + y_peers + [sibling]
    peers += [dev(z, rot(x, d, NX), y, 1 - k) for d in (2, 1, 3)]
    peers += [dev(z, x, rot(y, d, NX), 1 - k) for d in (2, 1, 3)]
    for peer in peers:
        pl.semaphore_signal(barrier, inc=1, device_id=peer, device_id_type=MESH)

    pairs = ((lad_hbm, lad), (mask_hbm, mask), (ve_hbm, ve), (oe_hbm, oe), (amp_hbm, amp), (drv_hbm, drv))
    loads = [pltpu.make_async_copy(src, dst, in_s.at[i]) for i, (src, dst) in enumerate(pairs)]
    for load in loads:
        load.start()

    eye = onehot(iota((64, 64), 0) == iota((64, 64), 1))
    spread = onehot((iota((O, 128), 1) & (O - 1)) == iota((O, 128), 0))
    group = iota((16, 128), 1) >> 5
    for load in loads[:4]:
        load.wait()
    keep = mask[p, lax.div(q, 2)].astype(F32)
    rows = lax.dot_general(
        eye, lad[...], (((1,), (1,)), ((), ())), preferred_element_type=F32
    ).astype(BF16)
    four = dot(rows, spread)
    packed = four[0:16]
    for t in range(1, 4):
        packed = jnp.where(group == t, four[16 * t : 16 * t + 16], packed)
    packed = (packed * keep).astype(BF16)
    blk[...] = packed
    G[zh, zl, k, x, y] = packed

    def copy(src, dst, ss, rs, to):
        return pltpu.make_async_remote_copy(
            src_ref=src, dst_ref=dst, send_sem=ss, recv_sem=rs, device_id=to, device_id_type=MESH
        )

    def wait_bytes(ref, sem):
        pltpu.make_async_copy(ref, ref, sem).wait()

    pl.semaphore_wait(barrier, len(peers))
    for d in reversed(NEAR):
        copy(blk, G.at[zh, zl, k, x, y], z_ss.at[d], z_rs.at[d], z_peer[d]).start()

    def plane(e):
        src_z = rot(z, NZ - e, NZ)
        return lax.div(src_z, NH), lax.rem(src_z, NH)

    def first(n):
        e = GROUPS[n]
        h_, l_ = plane(e)
        piece = G.at[h_, l_, k, x, y]
        if e:
            wait_bytes(blk, z_rs.at[e])
        if 1 <= e <= 4:
            copy(piece, piece, z_ss.at[e + 4], z_rs.at[e + 4], z_peer[4]).start()
        if 13 <= e <= 15:
            copy(piece, piece, z_ss.at[e - 4], z_rs.at[e - 4], z_peer[12]).start()
        for to in x_peers if n % 2 == 0 else y_peers:
            copy(piece, piece, f_ss, f_rs.at[n], to).start()

    def second(n):
        h_, l_ = plane(GROUPS[n])
        wait_bytes(G.at[0, 0, 0, 0, 0:3], f_rs.at[n])
        if n % 2 == 0:
            piece, to_all = G.at[h_, l_, k, :, y], y_peers
        else:
            piece, to_all = G.at[h_, l_, k, x], x_peers
        for to in to_all:
            copy(piece, piece, s_ss, s_rs.at[n], to).start()

    def third(n):
        h_, l_ = plane(GROUPS[n])
        wait_bytes(G.at[0, 0, 0, 0:3], s_rs.at[n])
        piece = G.at[h_, l_, k]
        copy(piece, piece, c_ss, c_rs.at[n], sibling).start()

    def use(n):
        if n % 2 == 0:
            return
        planes = [plane(GROUPS[m]) for m in (n - 1, n)]
        for m in (n - 1, n):
            wait_bytes(G.at[0, 0, 0], c_rs.at[m])
        wide = jnp.concatenate(
            [
                jnp.concatenate(
                    [G[h_, l_, j % 2, :, 2 * g + j // 2].reshape(64, 128) for j in range(4)], axis=1
                )
                for h_, l_ in planes
                for g in range(2)
            ],
            axis=0,
        )
        moved = dot(wide, shuf[...]).astype(BF16)
        for i, (h_, l_) in enumerate(planes):
            cols = pl.ds(pl.multiple_of(l_ * COLS, COLS), COLS)
            for t in range(4):
                W[pl.ds(h_ * NX, NX), t, :, cols] = jnp.concatenate(
                    [
                        moved[64 * (2 * i + g) : 64 * (2 * i + g) + 64, 128 * t : 128 * t + 128]
                        for g in range(2)
                    ],
                    axis=1,
                ).reshape(NX, 16, COLS)

    def prepare():
        r = iota((512, 512), 0)
        c = iota((512, 512), 1)
        shuf[...] = onehot(c == ((r >> 5) & 3) * 128 + (r >> 7) * 32 + (r & 31))
        loads[4].wait()
        ab[...] = amp[...].reshape(ROWS, IJ).astype(BF16)
        abt[...] = amp[...].astype(BF16)

        @pl.loop(0, 8)
        def _(i):
            r = iota((128, IJ), 0) + i * 128
            c = iota((128, IJ), 1)
            perm[pl.ds(pl.multiple_of(i * 128, 128), 128), :] = onehot(
                r == (c & (O - 1)) * O + (c >> 5)
            )

        lane = iota((8, IJ), 1)
        pair = jnp.zeros((8, IJ), F32)
        for i in range(O):
            e = oe[i]
            pair = pair + jnp.where((lane >> 5) == i, e, 0.0) + jnp.where((lane & (O - 1)) == i, e, 0.0)
        row = iota((8, IJ), 0)

        def over(first_b):
            base = -pair
            for b in range(8):
                base = base + jnp.where(row == b, ve[first_b + b], 0.0)
            return base

        base = over(q * 8)
        for a in range(16):
            rden[8 * a : 8 * a + 8, :] = 1.0 / (base + ve[p * 16 + a])
        for s in range(2):
            base = over(p * 16 + 8 * s)
            for a in range(EARLY):
                r = 8 * (s * EARLY + a)
                rden2[r : r + 8, :] = 1.0 / (base + ve[q * 8 + a])
        loads[5].wait()

    def give(src, dst, ss, rs, h):
        to = (lax.div(q, 2), 2 * p + h)
        own = jnp.logical_and(to[0] == p, to[1] == q)
        send = copy(src, dst, ss, rs, to)

        @pl.when(jnp.logical_not(own))
        def _():
            send.start()

        @pl.when(own)
        def _():
            pltpu.make_async_copy(src, dst, rs).start()

        def done():
            @pl.when(jnp.logical_not(own))
            def _():
                send.wait_send()

        return done

    given = []

    def early(_):
        for h in range(2):
            for j, (src, dst) in enumerate(((abt, araw), (drv, draw))):
                piece = src.at[8 * h : 8 * h + EARLY]
                given.append(give(piece, dst.at[k], r_ss.at[h, j], r_rs.at[k, j], h))

    steps = [first, second, third, use, early]
    for i, (kind, n) in enumerate(plan()):
        if i == 9:
            prepare()
        steps[kind](n)

    def columns(n):
        if isinstance(n, int):
            return slice(n * COLS, (n + 1) * COLS)
        return pl.ds(pl.multiple_of(n * COLS, COLS), COLS)

    def w_cols(n):
        return W[:, :, :, columns(n)].reshape(IJ, COLS)

    def halves(count, tile, drive, over_den, t_, b_, c_, two):
        for n in range(CHUNKS):
            t1 = dot(tile[...], w_cols(n))
            t_[:, columns(n)] = t1.astype(BF16)
            b1 = (drive(n) + t1) * over_den[:, columns(n)]
            high = b1.astype(BF16)
            b_[0:count, columns(n)] = high
            b_[count : 2 * count, columns(n)] = (b1 - high.astype(F32)).astype(BF16)

        for n in range(CHUNKS):
            turned = dot(t_[...], perm[:, columns(n)]) * over_den[:, columns(n)]
            c_[:, columns(n)] = turned.astype(BF16)

        for n in range(CHUNKS):
            two[:, columns(n)] = dot(c_[...], w_cols(n)).astype(BF16)

    def joined(n, count, b_, two):
        both = dot(b_[...], w_cols(n))
        return both[0:count] + both[count : 2 * count] + dot(two[...], perm[:, columns(n)])

    def drive(n):
        return drv[:, :, columns(n)].astype(F32).reshape(ROWS, COLS)

    halves(ROWS, ab, drive, rden, tb, lhs, cb, x2b)

    for n in range(CHUNKS):
        cols = slice(n * COLS, (n + 1) * COLS)
        zz = joined(n, ROWS, lhs, x2b)
        zsend[n] = zz.reshape(2, 8, 8, COLS).astype(BF16)
        for h in range(2):
            given.append(
                give(
                    zsend.at[n, h, EARLY:8], zrecv.at[n, k, EARLY:8], e_ss.at[n, h], e_rs.at[n, k], h
                )
            )
        x1[:, cols] = drv[:, :, cols].astype(F32).reshape(ROWS, COLS) + zz

    for s in range(2):
        for j, dst in enumerate((araw, draw)):
            wait_bytes(dst.at[s], r_rs.at[s, j])
    ab2[...] = araw[...].astype(F32).reshape(EROWS, IJ).astype(BF16)

    def early_drive(n):
        return draw[:, :, :, columns(n)].astype(F32).reshape(EROWS, COLS)

    halves(EROWS, ab2, early_drive, rden2, tb2, lhs2, cb2, x2b2)
    for n in range(CHUNKS):
        zz = joined(n, EROWS, lhs2, x2b2)
        zrecv[n, :, 0:EARLY] = zz.reshape(2, EARLY, 8, COLS).astype(BF16)

    for n in range(CHUNKS):
        for s in range(2):
            wait_bytes(zrecv.at[n, s, EARLY:8], e_rs.at[n, s])
        got = zrecv[n].astype(F32).reshape(ROWS, COLS).astype(BF16)
        for m in range(CHUNKS):
            turned = dot(got, perm[n * COLS : (n + 1) * COLS, m * COLS : (m + 1) * COLS])
            for c in range(COLS // 128):
                part = turned[:, 128 * c : 128 * c + 128]
                if n:
                    vs[m * (COLS // 128) + c] += part
                else:
                    vs[m * (COLS // 128) + c] = part

    @pl.loop(0, IJ // 128)
    def _(c):
        cols = pl.ds(pl.multiple_of(c * 128, 128), 128)
        for s in range(2):
            for b in range(8):
                r = 8 * (8 * s + b)
                other = vs[c, pl.ds(64 * s + b, 8, stride=8), :]
                out[8 * s + b, :, cols] = (x1[r : r + 8, cols] + other) * rden[r : r + 8, cols]

    for d in NEAR + GROUPS[9:]:
        wait_bytes(blk, z_ss.at[d])
    wait_bytes(G.at[0:3, :, 0, :, 0], f_ss)
    wait_bytes(G.at[0:3, :, 0], s_ss)
    wait_bytes(G.at[:, :, 0], c_ss)
    for done in given:
        done()


def on_device(amplitudes, driving, ladder, block_mask, virt_energy, occ_energy):
    vmem = pl.BlockSpec(memory_space=pltpu.VMEM)
    hbm = pl.BlockSpec(memory_space=pltpu.HBM)
    dma = pltpu.SemaphoreType.DMA
    return pl.pallas_call(
        kernel,
        out_shape=pltpu.VMEM(amplitudes.shape, F32),
        in_specs=[hbm] * 6,
        out_specs=vmem,
        scratch_shapes=[
            pltpu.VMEM((O, 64), BF16),
            pltpu.SMEM(block_mask.shape, jnp.int32),
            pltpu.SMEM(virt_energy.shape, F32),
            pltpu.SMEM(occ_energy.shape, F32),
            pltpu.VMEM((NH, NH, 2, NX, NX, 16, 128), BF16),
            pltpu.VMEM((16, 4, 16, IJ), BF16),
            pltpu.VMEM((IJ, IJ), BF16),
            pltpu.VMEM((512, 512), BF16),
            pltpu.VMEM((16, 128), BF16),
            pltpu.VMEM(amplitudes.shape, F32),
            pltpu.VMEM(driving.shape, BF16),
            pltpu.VMEM(amplitudes.shape, BF16),
            pltpu.VMEM((ROWS, IJ), F32),
            pltpu.VMEM((ROWS, IJ), BF16),
            pltpu.VMEM((ROWS, IJ), BF16),
            pltpu.VMEM((2 * ROWS, IJ), BF16),
            pltpu.VMEM((ROWS, IJ), BF16),
            pltpu.VMEM((ROWS, IJ), F32),
            pltpu.VMEM((ROWS, IJ), BF16),
            pltpu.VMEM((CHUNKS, 2, 8, 8, COLS), BF16),
            pltpu.VMEM((CHUNKS, 2, 8, 8, COLS), BF16),
            pltpu.VMEM((IJ // 128, ROWS, 128), F32),
            pltpu.VMEM((2, EARLY, 8, IJ), BF16),
            pltpu.VMEM((2, EARLY, 8, IJ), BF16),
            pltpu.VMEM((EROWS, IJ), F32),
            pltpu.VMEM((EROWS, IJ), BF16),
            pltpu.VMEM((EROWS, IJ), BF16),
            pltpu.VMEM((2 * EROWS, IJ), BF16),
            pltpu.VMEM((EROWS, IJ), BF16),
            pltpu.VMEM((EROWS, IJ), BF16),
            dma((6,)),
            dma((2, 2)),
            dma((2, 2)),
            dma((NZ,)),
            dma((NZ,)),
            dma(()),
            dma((NZ,)),
            dma(()),
            dma((NZ,)),
            dma(()),
            dma((NZ,)),
            dma((CHUNKS, 2)),
            dma((CHUNKS, 2)),
        ],
        compiler_params=pltpu.CompilerParams(collective_id=0, has_side_effects=True),
    )(amplitudes, driving, ladder.T, block_mask, virt_energy, occ_energy)


def solution(mesh):
    placed = (P("aa", "ba", None), P("aa", "ba", None), P("aa", "ba"), P(), P(), P())
    return jax.shard_map(
        on_device, mesh=mesh, in_specs=placed, out_specs=P("aa", "ba", None), check_vma=False
    )
```
